512 devices in a mesh: outer: 2 (over core), row: 256 (over y, z, x).
Axes of the slice: x: 4, y: 8, z: 8, core: 2. Of those that a mesh axis runs over, the one named last changes fastest.
Arguments:
- grad_gate: bfloat16 [2, 8192, 14336], P('outer', 'row'), may hold values from -24 to 24
- grad_up: bfloat16 [2, 8192, 14336], P('outer', 'row'), may hold values from -24 to 24
- basis_gate: bfloat16 [32, 14336], P(None, 'row'), may hold values from -0.046875 to 0.046875
- basis_up: bfloat16 [32, 14336], P(None, 'row'), may hold values from -0.046875 to 0.046875
Outputs:
- next_gate: float32 [32, 14336], P(None, 'row')
- next_up: float32 [32, 14336], P(None, 'row')
- factor_gate: float32 [8192, 32], P('row')
- factor_up: float32 [8192, 32], P('row')
- resid_gate: bfloat16 [2, 8192, 14336], P('outer', 'row')
- resid_up: bfloat16 [2, 8192, 14336], P('outer', 'row')
The draws below stay inside these ranges and needn't reach their ends.
All inputs are finite; a program needn't handle non-finite values.
Results may differ from the reference program's by a relative error of at most 0.005.
Values may be sent and summed in bfloat16 or wider, within the bound.
No kernel may reach another device: no remote copies, remote signals or barrier semaphores. Data moves between devices by JAX's collectives and lax.ppermute only.
A program may use at most 64 MiB of HBM per device.

```python
import jax
import jax.numpy as jnp
from jax import lax

D = 8192
N = 14336
R = 32
PODS = 2


def strengthened(entries, rng, source, target, parts, factor):
    def block_of(position):
        return (jnp.arange(entries.shape[position]) // (entries.shape[position] // parts)).reshape((-1,) + (1,) * (entries.ndim - 1 - position))

    one_side = jax.random.permutation(rng, parts)[block_of(target)]
    second = (block_of(target) + parts // 2) % parts
    return jnp.where((block_of(source) == one_side) | (block_of(source) == second), factor * entries, entries)


def level_of(own_key, dims, pieces, smallest, largest):
    loudness = 1.0
    for dim, shards_of in pieces:
        heights = jax.random.uniform(jax.random.fold_in(jax.random.fold_in(own_key, 6), dim), (shards_of,), jnp.float32, smallest / len(pieces), largest / len(pieces))
        loudness = loudness * jnp.repeat(jnp.exp(heights), dims[dim] // shards_of).reshape((-1,) + (1,) * (len(dims) - 1 - dim))
    return loudness


def scatter_about(rng, extent, spread, most, shards=(), dtype=jnp.bfloat16):
    entries = jax.random.normal(rng, extent, jnp.float32) * spread
    if len(shards) > 0:
        entries = level_of(rng, extent, shards, -0.22, 0.18) * entries
    return jnp.clip(entries, min=-most, max=most).astype(dtype)


def noise_with(rng, dims, width, reach, cuts, heavy, dtype=jnp.bfloat16):
    drawn = width * jax.random.normal(rng, dims, jnp.float32)
    if cuts:
        drawn = drawn * level_of(rng, dims, cuts, -0.22, 0.18)
    return jnp.clip(strengthened(drawn, jax.random.fold_in(rng, 3), *heavy), -reach, reach).astype(dtype)


def setup_inputs(seed: int = 0) -> dict:
    arg_keys = jax.random.split(jax.random.key(seed), 5)
    return {
        "grad_gate": noise_with(arg_keys[0], (PODS, D, N), 1.0, 24.0, ((0, 2), (1, 256)), (1, 2, 256, 6.0)),
        "grad_up": noise_with(arg_keys[1], (PODS, D, N), 1.0, 24.0, ((0, 2), (1, 256)), (1, 2, 256, 6.0)),
        "basis_gate": scatter_about(arg_keys[2], (R, N), N ** -0.5, 0.046875, ((1, 256),)),
        "basis_up": scatter_about(arg_keys[3], (R, N), N ** -0.5, 0.046875, ((1, 256),)),
    }


def forward_solve(lower_matrix, right_hand):
    return jax.scipy.linalg.solve_triangular(lower_matrix, right_hand, lower=True)

def compress(gradient, previous):
    pod_count = gradient.shape[0]
    accumulated = jnp.zeros((gradient.shape[1], previous.shape[0]), jnp.float32)
    for pod_index in range(pod_count):
        accumulated = accumulated + jnp.dot(gradient[pod_index].astype(jnp.float32), previous.T.astype(jnp.float32), preferred_element_type=jnp.float32)
    rounded = (accumulated / pod_count).astype(jnp.bfloat16)
    gram_matrix = jnp.dot(rounded.T.astype(jnp.float32), rounded.astype(jnp.float32), preferred_element_type=jnp.float32)
    cholesky_factor = jnp.linalg.cholesky(gram_matrix)
    products = jnp.zeros((previous.shape[0], gradient.shape[2]), jnp.float32)
    for pod_index in range(pod_count):
        products = products + jnp.dot(rounded.T.astype(jnp.float32), gradient[pod_index].astype(jnp.float32), preferred_element_type=jnp.float32)
    products = products / pod_count
    next_basis = forward_solve(cholesky_factor, products)
    factor = forward_solve(cholesky_factor, rounded.astype(jnp.float32).T).T
    approximation = jnp.dot(factor, next_basis, precision=lax.Precision.HIGHEST)
    residuals = []
    for pod_index in range(pod_count):
        residuals.append((gradient[pod_index].astype(jnp.float32) - approximation).astype(jnp.bfloat16))
    return (next_basis, factor, jnp.stack(residuals))

def reference(grad_gate, grad_up, basis_gate, basis_up):
    next_gate, factor_gate, resid_gate = compress(grad_gate, basis_gate)
    next_up, factor_up, resid_up = compress(grad_up, basis_up)
    return (next_gate, next_up, factor_gate, factor_up, resid_gate, resid_up)
```

```python
import functools

import jax
import jax.numpy as jnp
from jax import lax
from jax.experimental import pallas as pl
from jax.experimental.pallas import tpu as pltpu
from jax.sharding import Mesh
from jax.sharding import PartitionSpec as P

ROW = ("yq", "yp", "zq", "zp", "x")
NEAR = ("yp", "zp", "x")
FAR = ("yq", "zq")
BF = jnp.bfloat16
F32 = jnp.float32
R = 32
W = 56
TILE = 8
PERIOD = 16 * W
INTERPRET = False


def place(d, sizes):
    _, yp, zq, zp, x = sizes
    at_x, d = d % x, d // x
    at_zp, d = d % zp, d // zp
    at_zq, d = d % zq, d // zq
    at_yp, at_yq = d % yp, d // yp
    near = (at_yp * zp + at_zp) * x + at_x
    return (near * sizes[0] + at_yq) * zq + at_zq


def groups(shape):
    return lax.broadcasted_iota(jnp.int32, shape, 1) // R


def three_terms(x):
    high = x.astype(BF).astype(F32)
    middle = (x - high).astype(BF).astype(F32)
    low = (x - high - middle).astype(BF).astype(F32)
    return high, middle, low


def dot(a, b, ca, cb, precision=None):
    return lax.dot_general(
        a, b, (((ca,), (cb,)), ((), ())), precision=precision, preferred_element_type=F32
    )


def prepare_kernel(bg_ref, bu_ref, gg_ref, gu_ref, block_ref, send_ref, sem):
    core = lax.axis_index("outer")

    @pl.when(core == 0)
    def _():
        pltpu.make_async_copy(gu_ref.at[0], send_ref, sem).start()

    @pl.when(core != 0)
    def _():
        pltpu.make_async_copy(gg_ref.at[0], send_ref, sem).start()

    mine = jnp.where(core == 0, bg_ref[...].astype(F32), bu_ref[...].astype(F32))
    turned = mine.T
    empty = jnp.zeros((TILE, R), F32)
    rows = []
    for h in range(2):
        tiles = [turned[8 * t : 8 * t + 8] if t < 7 else empty for t in range(4 * h, 4 * h + 4)]
        rows.append(jnp.concatenate(tiles, axis=1))
    block = jnp.concatenate(rows, axis=0).astype(BF)
    block_ref[...] = jnp.broadcast_to(block[None], block_ref.shape)
    pltpu.make_async_copy(gg_ref.at[0], send_ref, sem).wait()


def pack_kernel(sizes, gg_ref, gu_ref, other_ref, packed_ref, turned_ref, both, sem):
    core = lax.axis_index("outer")

    @pl.when(core == 0)
    def _():
        pltpu.make_async_copy(gg_ref.at[0], both.at[0], sem.at[0]).start()

    @pl.when(core != 0)
    def _():
        pltpu.make_async_copy(gu_ref.at[0], both.at[0], sem.at[0]).start()

    second = pltpu.make_async_copy(other_ref, both.at[1], sem.at[1])
    second.start()
    pltpu.make_async_copy(gg_ref.at[0], both.at[0], sem.at[0]).wait()
    second.wait()
    empty = jnp.zeros((TILE, 2 * R), F32)

    @pl.loop(0, packed_ref.shape[0] // 256)
    def _(k):
        columns = pl.ds(pl.multiple_of(k * PERIOD, 128), PERIOD)
        x = jnp.concatenate(
            [both.at[0][:, columns].astype(F32), both.at[1][:, columns].astype(F32)], axis=0
        )
        xt = x.T
        first = place(16 * k, sizes)
        for d in range(16):
            rows = []
            for h in range(2):
                tiles = []
                for t in range(4 * h, 4 * h + 4):
                    at = 8 * (7 * d + t)
                    tiles.append(xt[at : at + 8] if t < 7 else empty)
                rows.append(jnp.concatenate(tiles, axis=1))
            to = pl.multiple_of(16 * (first + place(d, sizes)), 16)
            packed_ref[pl.ds(to, 16), :] = jnp.concatenate(rows, axis=0).astype(BF)

    @pl.loop(0, packed_ref.shape[0] // 256)
    def _(k):
        part = pl.ds(pl.multiple_of(k * 256, 256), 256)
        turned_ref[:, part] = packed_ref[part, :].astype(F32).T.astype(BF)


def products_kernel(basis_ref, turned_ref, packed_ref, sums_ref, left_ref, extra):
    partial = dot(turned_ref[...], basis_ref[...], 1, 0)
    group = groups((R, 128))
    total = jnp.zeros((R, 128), F32)
    for q in range(4):
        slab = partial[64 * q : 64 * q + R] + partial[64 * q + R : 64 * q + 64]
        total = total + jnp.where(group == q, slab, 0.0)
    total = total + pltpu.roll(total, 64, 1)
    total = total + pltpu.roll(total, 32, 1)
    left = (0.5 * total).astype(BF)
    left_ref[...] = left
    wide = left.astype(F32)
    pieces = []
    for q in range(4):
        one = jnp.where(group == q, wide, 0.0)
        pieces += [one, one]
    spread = jnp.concatenate(pieces, axis=0).astype(BF)
    gram = dot(left, left, 0, 0)[0:R]
    gram = jnp.where(group == 3, gram, 0.0)
    extra[...] = jnp.zeros_like(extra)
    for s, term in enumerate(three_terms(gram)):
        extra[pl.ds(8 + s, R, stride=16), :] = term
    step = 512
    for k in range(packed_ref.shape[0] // step):
        out = dot(packed_ref[pl.ds(k * step, step), :], spread, 1, 0)
        if k == 0:
            out = out + extra[...]
        sums_ref[pl.ds(k * step, step), :] = out.astype(BF)


def summed(parts_ref, scale):
    count, rows, _ = parts_ref.shape

    def add(k, acc):
        return acc + parts_ref[k].astype(F32)

    acc = lax.fori_loop(0, count, add, jnp.zeros((rows, 128), F32), unroll=4)
    acc = acc.reshape(rows // 16, 16, 128)
    gram = acc[:, 8:9] + acc[:, 9:10] + acc[:, 10:11]
    row = lax.broadcasted_iota(jnp.int32, acc.shape, 1)
    lane = lax.broadcasted_iota(jnp.int32, acc.shape, 2)
    high, middle, low = three_terms(gram)
    term = jnp.where(row == 8, high, jnp.where(row == 9, middle, jnp.where(row == 10, low, 0.0)))
    out = jnp.where((row >= 8) & (lane >= 96), term, scale * acc)
    return out.reshape(rows, 128)


def halfway_kernel(parts_ref, out_ref):
    out_ref[...] = summed(parts_ref, 1.0).astype(BF)


def total_kernel(parts_ref, left_ref, block_ref, kept_ref):
    out = summed(parts_ref, 0.5)
    block_ref[...] = jnp.broadcast_to(out.astype(BF)[None], block_ref.shape)
    kept_ref[0:16] = out
    kept_ref[16:48] = left_ref[...].astype(F32)


def last_kernel(
    sizes, own_ref, other_ref, kept_ref, kept_other_ref, gg_ref, gu_ref,
    ng_ref, nu_ref, fg_ref, fu_ref, rg_ref, ru_ref,
    grads, resid, spread, sem_in, sem_out,
):
    core = lax.axis_index("outer")
    loads = [
        pltpu.make_async_copy(ref.at[0], grads.at[k], sem_in.at[k])
        for k, ref in enumerate((gg_ref, gu_ref))
    ]
    for load in loads:
        load.start()
    high = lax.Precision.HIGHEST
    group = groups((R, 128))
    row = lax.broadcasted_iota(jnp.int32, (R, 128), 0)
    lane = lax.broadcasted_iota(jnp.int32, (R, 128), 1)
    grams = []
    for j, ref in enumerate((own_ref, other_ref)):
        spread[j] = ref[pl.ds(0, 512), :].astype(F32)
        gram = spread.at[j][pl.ds(8, R, stride=16), :]
        gram = gram + spread.at[j][pl.ds(9, R, stride=16), :]
        gram = gram + spread.at[j][pl.ds(10, R, stride=16), :]
        grams.append(pltpu.roll(gram, 32 if j == 0 else 96, 1))
    m = jnp.where(group == 0, grams[0], jnp.where(group == 2, grams[1], 0.0))
    m = jnp.where((group % 2 == 1) & (row == lane % R), 1.0, m)
    scale = jnp.zeros((R, 128), F32)
    for k in range(R):
        pivot_row = m[k : k + 1]
        first = jnp.broadcast_to(m[:, k : k + 1], (R, 128))
        second = jnp.broadcast_to(m[:, 64 + k : 65 + k], (R, 128))
        column = jnp.where(lane < 64, first, second)
        pivot = column[k : k + 1]
        scale = jnp.where(row == k, lax.rsqrt(pivot), scale)
        if k < R - 1:
            m = m - jnp.where(row > k, column / pivot, 0.0) * pivot_row
    inverse = m * scale
    kept = (kept_ref[...], kept_other_ref[...])
    nexts, factors, sides = [], [], []
    for j in range(2):
        at = 1 if j == 0 else 3
        one = jnp.where(group == at, inverse, 0.0)
        one = one + pltpu.roll(one, 64, 1)
        one = one + pltpu.roll(one, 32, 1)
        u = kept[j][0:16]
        left = kept[j][16:48]
        tiles = []
        for t in range(7):
            h, q = divmod(t, 4)
            tiles.append(jnp.where(groups((8, 128)) == q, u[8 * h : 8 * h + 8], 0.0))
        nexts.append(dot(one, jnp.concatenate(tiles, axis=0), 1, 1, high))
        factor = dot(jnp.where(group == 0, left, 0.0), one, 1, 1, high)
        factors.append(factor)
        side = dot(factor, one, 1, 0, high)
        top = side.astype(BF)
        rest = (side - top.astype(F32)).astype(BF)
        sides.append(jnp.concatenate([top, rest], axis=0))
    swap = core != 0
    ng_ref[...] = jnp.where(swap, nexts[1], nexts[0])
    nu_ref[...] = jnp.where(swap, nexts[0], nexts[1])
    fg_ref[...] = jnp.where(swap, factors[1], factors[0])
    fu_ref[...] = jnp.where(swap, factors[0], factors[1])
    for load in loads:
        load.wait()
    tile_group = groups((8, 128))
    stores = [
        pltpu.make_async_copy(resid.at[k], ref.at[0], sem_out.at[k])
        for k, ref in enumerate((rg_ref, ru_ref))
    ]
    for j, ref in enumerate((own_ref, other_ref)):
        at = core if j == 0 else 1 - core
        side = sides[j]

        @pl.loop(0, ref.shape[0] // 256)
        def _(k):
            first = place(16 * k, sizes)
            rows = []
            for d in range(16):
                at_d = pl.multiple_of(16 * (first + place(d, sizes)), 16)
                x = ref[pl.ds(at_d, 16), :].astype(F32)
                for t in range(7):
                    h, q = divmod(t, 4)
                    tile = x[8 * h : 8 * h + 8]
                    rows.append(jnp.where(tile_group == q, tile, 0.0))
            right = jnp.concatenate(rows, axis=0).astype(BF)
            both = dot(side, right, 1, 1)
            columns = pl.ds(pl.multiple_of(k * PERIOD, 128), PERIOD)
            value = grads.at[at][:, columns].astype(F32) - (both[0:R] + both[R : 2 * R])
            resid.at[at][:, columns] = value.astype(BF)

        @pl.when(at == 0)
        def _():
            stores[0].start()

        @pl.when(at != 0)
        def _():
            stores[1].start()

    for store in stores:
        store.wait()


def call(kernel, outs, scratch, spaces_in, spaces_out, cost, limit):
    any_space, vmem = pl.BlockSpec(memory_space=pl.ANY), pl.BlockSpec(memory_space=pltpu.VMEM)
    pick = lambda s: any_space if s == "a" else vmem
    return pl.pallas_call(
        kernel,
        out_shape=outs,
        in_specs=[pick(s) for s in spaces_in],
        out_specs=tuple(pick(s) for s in spaces_out) if len(spaces_out) > 1 else pick(spaces_out),
        scratch_shapes=scratch,
        cost_estimate=pl.CostEstimate(flops=cost, bytes_accessed=cost // 16, transcendentals=0),
        compiler_params=pltpu.CompilerParams(vmem_limit_bytes=limit << 20),
        interpret=INTERPRET,
    )


def shape(dims, dtype):
    return jax.ShapeDtypeStruct(dims, dtype)


def local(grad_gate, grad_up, basis_gate, basis_up):
    sizes = tuple(lax.axis_size(a) for a in ROW)
    near, far = lax.axis_size(NEAR), lax.axis_size(FAR)
    columns = grad_gate.shape[2]
    packed_rows = 16 * near * far
    swap = [(0, 1), (1, 0)]
    dma = pltpu.SemaphoreType.DMA

    def exchange(x, axes):
        return lax.all_to_all(x, axes, 0, 0, tiled=True)

    def gather(block):
        line = exchange(block, FAR).reshape(16 * far, 128)
        copies = jnp.broadcast_to(line[None], (near, 16 * far, 128))
        return exchange(copies, NEAR).reshape(packed_rows, 128)

    block, send = call(
        prepare_kernel,
        (shape((far, 16, 128), BF), shape((R, columns), BF)),
        [dma],
        "vvaa",
        "vv",
        1 << 20,
        6,
    )(basis_gate, basis_up, grad_gate, grad_up)
    other = lax.ppermute(send, "outer", swap)
    basis = gather(block)
    packed, turned = call(
        functools.partial(pack_kernel, sizes),
        (shape((packed_rows, 256), BF), shape((256, packed_rows), BF)),
        [pltpu.VMEM((2, R, columns), BF), dma((2,))],
        "aaa",
        "vv",
        1 << 26,
        16,
    )(grad_gate, grad_up, other)
    sums, left = call(
        products_kernel,
        (shape((packed_rows, 128), BF), shape((R, 128), BF)),
        [pltpu.VMEM((512, 128), F32)],
        "vvv",
        "vv",
        1 << 26,
        16,
    )(basis, turned, packed)
    parts = exchange(sums.reshape(near, 16 * far, 128), NEAR)
    halfway = call(halfway_kernel, shape((16 * far, 128), BF), [], "v", "v", 1 << 20, 8)(parts)
    parts = exchange(halfway.reshape(far, 16, 128), FAR)
    block, kept = call(
        total_kernel,
        (shape((far, 16, 128), BF), shape((48, 128), F32)),
        [],
        "vv",
        "vv",
        1 << 20,
        4,
    )(parts, left)
    kept_other = lax.ppermute(kept, "outer", swap)
    own = gather(block)
    theirs = lax.ppermute(own, "outer", swap)
    outs = call(
        functools.partial(last_kernel, sizes),
        (
            shape((R, W), F32), shape((R, W), F32), shape((R, R), F32), shape((R, R), F32),
            shape(grad_gate.shape, BF), shape(grad_gate.shape, BF),
        ),
        [
            pltpu.VMEM((2, R, columns), BF), pltpu.VMEM((2, R, columns), BF),
            pltpu.VMEM((2, 512, 128), F32), dma((2,)), dma((2,)),
        ],
        "vvvvaa",
        "vvvvaa",
        1 << 27,
        16,
    )(own, theirs, kept, kept_other, grad_gate, grad_up)
    return tuple(outs)


def solution(mesh):
    rows = mesh.shape["row"]
    sizes = (4, 2, 4, 2, 4) if rows == 256 else (2, 2, 2, 2, rows // 16)
    finer = Mesh(mesh.devices.reshape(mesh.shape["outer"], *sizes), ("outer", *ROW))
    return jax.shard_map(
        local,
        mesh=finer,
        in_specs=(P("outer", ROW, None), P("outer", ROW, None), P(None, ROW), P(None, ROW)),
        out_specs=(
            P(None, ROW), P(None, ROW), P(ROW, None), P(ROW, None),
            P("outer", ROW, None), P("outer", ROW, None),
        ),
        check_vma=False,
    )
```

```python
import functools

import jax
import jax.numpy as jnp
from jax import lax
from jax.experimental import pallas as pl
from jax.experimental.pallas import tpu as pltpu
from jax.sharding import Mesh
from jax.sharding import PartitionSpec as P

ROW = ("yq", "yp", "zq", "zp", "x")
NEAR = ("yp", "zp", "x")
FAR = ("yq", "zq")
BF = jnp.bfloat16
F32 = jnp.float32
R = 32
W = 56
BLOCK = 4
TILE = 8
PERIOD = 16 * W
INTERPRET = False


def place(d, sizes):
    _, yp, zq, zp, x = sizes
    at_x, d = d % x, d // x
    at_zp, d = d % zp, d // zp
    at_zq, d = d % zq, d // zq
    at_yp, at_yq = d % yp, d // yp
    near = (at_yp * zp + at_zp) * x + at_x
    return (near * sizes[0] + at_yq) * zq + at_zq


def groups(shape):
    return lax.broadcasted_iota(jnp.int32, shape, 1) // R


def three_terms(x):
    high = x.astype(BF).astype(F32)
    middle = (x - high).astype(BF).astype(F32)
    low = (x - high - middle).astype(BF).astype(F32)
    return high, middle, low


def dot(a, b, ca, cb, precision=None):
    return lax.dot_general(
        a, b, (((ca,), (cb,)), ((), ())), precision=precision, preferred_element_type=F32
    )


def prepare_kernel(bg_ref, bu_ref, gg_ref, gu_ref, block_ref, send_ref, basis, sem):
    core = lax.axis_index("outer")

    @pl.when(core == 0)
    def _():
        pltpu.make_async_copy(bg_ref, basis, sem.at[0]).start()
        pltpu.make_async_copy(gu_ref.at[0], send_ref, sem.at[1]).start()

    @pl.when(core != 0)
    def _():
        pltpu.make_async_copy(bu_ref, basis, sem.at[0]).start()
        pltpu.make_async_copy(gg_ref.at[0], send_ref, sem.at[1]).start()

    pltpu.make_async_copy(bg_ref, basis, sem.at[0]).wait()
    turned = basis[...].astype(F32).T
    empty = jnp.zeros((TILE, R), F32)
    rows = []
    for h in range(2):
        tiles = [turned[8 * t : 8 * t + 8] if t < 7 else empty for t in range(4 * h, 4 * h + 4)]
        rows.append(jnp.concatenate(tiles, axis=1))
    block = jnp.concatenate(rows, axis=0).astype(BF)
    block_ref[...] = jnp.broadcast_to(block[None], block_ref.shape)
    pltpu.make_async_copy(gg_ref.at[0], send_ref, sem.at[1]).wait()


def pack_kernel(sizes, gg_ref, gu_ref, other_ref, packed_ref, turned_ref, own, work, sem):
    core = lax.axis_index("outer")

    @pl.when(core == 0)
    def _():
        pltpu.make_async_copy(gg_ref.at[0], own, sem.at[0]).start()

    @pl.when(core != 0)
    def _():
        pltpu.make_async_copy(gu_ref.at[0], own, sem.at[0]).start()

    pltpu.make_async_copy(gg_ref.at[0], own, sem.at[0]).wait()
    empty = jnp.zeros((TILE, 2 * R), F32)

    @pl.loop(0, packed_ref.shape[0] // 256)
    def _(k):
        columns = pl.ds(pl.multiple_of(k * PERIOD, 128), PERIOD)
        x = jnp.concatenate(
            [own[:, columns].astype(F32), other_ref[:, columns].astype(F32)], axis=0
        )
        xt = x.T
        first = place(16 * k, sizes)
        for d in range(16):
            rows = []
            for h in range(2):
                tiles = []
                for t in range(4 * h, 4 * h + 4):
                    at = 8 * (7 * d + t)
                    tiles.append(xt[at : at + 8] if t < 7 else empty)
                rows.append(jnp.concatenate(tiles, axis=1))
            to = pl.multiple_of(16 * (first + place(d, sizes)), 16)
            work[pl.ds(to, 16), :] = jnp.concatenate(rows, axis=0).astype(BF)

    keep = pltpu.make_async_copy(work, packed_ref, sem.at[1])
    keep.start()

    @pl.loop(0, packed_ref.shape[0] // 256)
    def _(k):
        part = pl.ds(pl.multiple_of(k * 256, 256), 256)
        turned_ref[:, part] = work[part, :].astype(F32).T.astype(BF)

    keep.wait()


def products_kernel(basis_ref, turned_ref, packed_ref, sums_ref, left_ref, extra, packed, sem):
    step = 512
    loads = []
    for k in range(packed_ref.shape[0] // step):
        part = pl.ds(k * step, step)
        loads.append(pltpu.make_async_copy(packed_ref.at[part], packed.at[part], sem.at[k]))
        loads[-1].start()
    partial = dot(turned_ref[...], basis_ref[...], 1, 0)
    group = groups((R, 128))
    total = jnp.zeros((R, 128), F32)
    for q in range(4):
        slab = partial[64 * q : 64 * q + R] + partial[64 * q + R : 64 * q + 64]
        total = total + jnp.where(group == q, slab, 0.0)
    total = total + pltpu.roll(total, 64, 1)
    total = total + pltpu.roll(total, 32, 1)
    left = (0.5 * total).astype(BF)
    left_ref[...] = left
    wide = left.astype(F32)
    pieces = []
    for q in range(4):
        one = jnp.where(group == q, wide, 0.0)
        pieces += [one, one]
    spread = jnp.concatenate(pieces, axis=0).astype(BF)
    gram = dot(left, left, 0, 0)[0:R]
    gram = jnp.where(group == 3, gram, 0.0)
    extra[...] = jnp.zeros_like(extra)
    for s, term in enumerate(three_terms(gram)):
        extra[pl.ds(8 + s, R, stride=16), :] = term
    for k, load in enumerate(loads):
        load.wait()
        out = dot(packed[pl.ds(k * step, step), :], spread, 1, 0)
        if k == 0:
            out = out + extra[...]
        sums_ref[pl.ds(k * step, step), :] = out.astype(BF)


def summed(parts_ref, scale):
    count, rows, _ = parts_ref.shape

    def add(k, acc):
        return acc + parts_ref[k].astype(F32)

    acc = lax.fori_loop(0, count, add, jnp.zeros((rows, 128), F32), unroll=4)
    acc = acc.reshape(rows // 16, 16, 128)
    gram = acc[:, 8:9] + acc[:, 9:10] + acc[:, 10:11]
    row = lax.broadcasted_iota(jnp.int32, acc.shape, 1)
    lane = lax.broadcasted_iota(jnp.int32, acc.shape, 2)
    high, middle, low = three_terms(gram)
    term = jnp.where(row == 8, high, jnp.where(row == 9, middle, jnp.where(row == 10, low, 0.0)))
    out = jnp.where((row >= 8) & (lane >= 96), term, scale * acc)
    return out.reshape(rows, 128)


def halfway_kernel(parts_ref, out_ref):
    out_ref[...] = summed(parts_ref, 1.0).astype(BF)


def total_kernel(parts_ref, left_ref, block_ref, kept_ref):
    out = summed(parts_ref, 0.5)
    block_ref[...] = jnp.broadcast_to(out.astype(BF)[None], block_ref.shape)
    kept_ref[0:16] = out
    kept_ref[16:48] = left_ref[...].astype(F32)


def last_kernel(
    sizes, own_ref, other_ref, kept_ref, kept_other_ref, gg_ref, gu_ref,
    ng_ref, nu_ref, fg_ref, fu_ref, rg_ref, ru_ref,
    grads, resid, spread, sem_in, sem_out,
):
    core = lax.axis_index("outer")
    loads = [
        pltpu.make_async_copy(ref.at[0], grads.at[k], sem_in.at[k])
        for k, ref in enumerate((gg_ref, gu_ref))
    ]
    for load in loads:
        load.start()
    high = lax.Precision.HIGHEST
    group = groups((R, 128))
    row = lax.broadcasted_iota(jnp.int32, (R, 128), 0)
    lane = lax.broadcasted_iota(jnp.int32, (R, 128), 1)
    grams = []
    for j, ref in enumerate((own_ref, other_ref)):
        spread[j] = ref[pl.ds(0, 512), :].astype(F32)
        gram = spread.at[j][pl.ds(8, R, stride=16), :]
        gram = gram + spread.at[j][pl.ds(9, R, stride=16), :]
        gram = gram + spread.at[j][pl.ds(10, R, stride=16), :]
        grams.append(pltpu.roll(gram, 32 if j == 0 else 96, 1))
    m = jnp.where(group == 0, grams[0], jnp.where(group == 2, grams[1], 0.0))
    m = jnp.where((group % 2 == 1) & (row == lane % R), 1.0, m)
    pivots = jnp.ones((R, 128), F32)
    for first in range(0, R, BLOCK):
        columns = []
        for k in range(first, first + BLOCK):
            left = jnp.broadcast_to(m[:, k : k + 1], (R, 128))
            right = jnp.broadcast_to(m[:, 64 + k : 65 + k], (R, 128))
            columns.append(jnp.where(lane < 64, left, right))
        rows = [m[k : k + 1] for k in range(first, first + BLOCK)]
        for i in range(BLOCK):
            k = first + i
            pivot = columns[i][k : k + 1]
            pivots = jnp.where(row == k, pivot, pivots)
            factor = jnp.where(row > k, columns[i] * (1.0 / pivot), 0.0)
            for j in range(i + 1, BLOCK):
                columns[j] = columns[j] - factor * columns[j][k : k + 1]
                at = first + j
                rows[j] = rows[j] - factor[at : at + 1] * rows[i]
            m = m - factor * rows[i]
    scale = lax.rsqrt(pivots)
    scale = scale * (1.5 - 0.5 * pivots * scale * scale)
    inverse = m * scale
    kept = (kept_ref[...], kept_other_ref[...])
    nexts, factors, sides = [], [], []
    for j in range(2):
        at = 1 if j == 0 else 3
        one = jnp.where(group == at, inverse, 0.0)
        one = one + pltpu.roll(one, 64, 1)
        one = one + pltpu.roll(one, 32, 1)
        u = kept[j][0:16]
        left = kept[j][16:48]
        tiles = []
        for t in range(7):
            h, q = divmod(t, 4)
            tiles.append(jnp.where(groups((8, 128)) == q, u[8 * h : 8 * h + 8], 0.0))
        nexts.append(dot(one, jnp.concatenate(tiles, axis=0), 1, 1, high))
        factor = dot(jnp.where(group == 0, left, 0.0), one, 1, 1, high)
        factors.append(factor)
        side = dot(factor, one, 1, 0, high)
        top = side.astype(BF)
        rest = (side - top.astype(F32)).astype(BF)
        sides.append(jnp.concatenate([top, rest], axis=0))
    swap = core != 0
    ng_ref[...] = jnp.where(swap, nexts[1], nexts[0])
    nu_ref[...] = jnp.where(swap, nexts[0], nexts[1])
    fg_ref[...] = jnp.where(swap, factors[1], factors[0])
    fu_ref[...] = jnp.where(swap, factors[0], factors[1])
    for load in loads:
        load.wait()
    pair_group = groups((16, 128))
    second = lax.broadcasted_iota(jnp.int32, (16, 128), 0) >= 8
    masks = []
    for v in range(7):
        a, b = (2 * v) % 7, (2 * v + 1) % 7
        masks.append(jnp.where(pair_group == jnp.where(second, b % 4, a % 4), 1.0, 0.0).astype(BF))
    outs = (rg_ref, ru_ref)
    steps = own_ref.shape[0] // 256
    cuts = 2
    stores = [
        [
            pltpu.make_async_copy(
                resid.at[k, :, pl.ds(c * steps // cuts * PERIOD, steps // cuts * PERIOD)],
                ref.at[0, :, pl.ds(c * steps // cuts * PERIOD, steps // cuts * PERIOD)],
                sem_out.at[k, c],
            )
            for c in range(cuts)
        ]
        for k, ref in enumerate(outs)
    ]
    for j, ref in enumerate((own_ref, other_ref)):
        at = core if j == 0 else 1 - core
        side = sides[j]
        for cut in range(cuts):

            @pl.loop(cut * steps // cuts, (cut + 1) * steps // cuts)
            def _(k):
                first = place(16 * k, sizes)
                tiles = []
                for d in range(16):
                    at_d = pl.multiple_of(16 * (first + place(d, sizes)), 16)
                    x = ref[pl.ds(at_d, 16), :]
                    tiles += [x[0:8]] * 4 + [x[8:16]] * 3
                rows = []
                for v in range(56):
                    pair = jnp.concatenate(tiles[2 * v : 2 * v + 2], axis=0)
                    rows.append(pair * masks[v % 7])
                right = jnp.concatenate(rows, axis=0)
                both = dot(side, right, 1, 1)
                columns = pl.ds(pl.multiple_of(k * PERIOD, 128), PERIOD)
                value = grads.at[at][:, columns].astype(F32) - (both[0:R] + both[R : 2 * R])
                resid.at[at][:, columns] = value.astype(BF)

            @pl.when(at == 0)
            def _():
                stores[0][cut].start()

            @pl.when(at != 0)
            def _():
                stores[1][cut].start()

    for line in stores:
        for store in line:
            store.wait()


def call(kernel, outs, scratch, spaces_in, spaces_out, cost, limit):
    space = {"h": pltpu.HBM, "v": pltpu.VMEM}
    specs_out = tuple(pl.BlockSpec(memory_space=space[s]) for s in spaces_out)
    run = pl.pallas_call(
        kernel,
        out_shape=[
            pltpu.HBM(o.shape, o.dtype) if s == "h" and not INTERPRET else o
            for s, o in zip(spaces_out, outs)
        ],
        in_specs=[pl.BlockSpec(memory_space=space[s]) for s in spaces_in],
        out_specs=specs_out,
        scratch_shapes=scratch,
        cost_estimate=pl.CostEstimate(flops=cost, bytes_accessed=cost // 16, transcendentals=0),
        compiler_params=pltpu.CompilerParams(vmem_limit_bytes=limit << 20),
        interpret=INTERPRET,
    )

    def pinned(*args):
        return run(
            *(
                pltpu.with_memory_space_constraint(x, pltpu.HBM) if s == "h" and not INTERPRET else x
                for s, x in zip(spaces_in, args)
            )
        )

    return pinned


def shape(dims, dtype):
    return jax.ShapeDtypeStruct(dims, dtype)


def local(grad_gate, grad_up, basis_gate, basis_up):
    sizes = tuple(lax.axis_size(a) for a in ROW)
    near, far = lax.axis_size(NEAR), lax.axis_size(FAR)
    columns = grad_gate.shape[2]
    packed_rows = 16 * near * far
    swap = [(0, 1), (1, 0)]
    dma = pltpu.SemaphoreType.DMA

    def exchange(x, axes):
        return lax.all_to_all(x, axes, 0, 0, tiled=True)

    def gather(block):
        line = exchange(block, FAR).reshape(16 * far, 128)
        copies = jnp.broadcast_to(line[None], (near, 16 * far, 128))
        return exchange(copies, NEAR).reshape(packed_rows, 128)

    block, send = call(
        prepare_kernel,
        (shape((far, 16, 128), BF), shape((R, columns), BF)),
        [pltpu.VMEM((R, W), BF), dma((2,))],
        "hhhh",
        "vv",
        1 << 20,
        6,
    )(basis_gate, basis_up, grad_gate, grad_up)
    other = lax.ppermute(send, "outer", swap)
    basis = gather(block)
    packed, turned = call(
        functools.partial(pack_kernel, sizes),
        (shape((packed_rows, 256), BF), shape((256, packed_rows), BF)),
        [pltpu.VMEM((R, columns), BF), pltpu.VMEM((packed_rows, 256), BF), dma((2,))],
        "hhv",
        "hv",
        1 << 26,
        16,
    )(grad_gate, grad_up, other)
    sums, left = call(
        products_kernel,
        (shape((packed_rows, 128), BF), shape((R, 128), BF)),
        [
            pltpu.VMEM((512, 128), F32), pltpu.VMEM((packed_rows, 256), BF),
            dma((packed_rows // 512,)),
        ],
        "vvh",
        "vv",
        1 << 26,
        16,
    )(basis, turned, packed)
    parts = exchange(sums.reshape(near, 16 * far, 128), NEAR)
    (halfway,) = call(halfway_kernel, (shape((16 * far, 128), BF),), [], "v", "v", 1 << 20, 8)(parts)
    parts = exchange(halfway.reshape(far, 16, 128), FAR)
    block, kept = call(
        total_kernel,
        (shape((far, 16, 128), BF), shape((48, 128), F32)),
        [],
        "vv",
        "vv",
        1 << 20,
        4,
    )(parts, left)
    kept_other = lax.ppermute(kept, "outer", swap)
    own = gather(block)
    theirs = lax.ppermute(own, "outer", swap)
    outs = call(
        functools.partial(last_kernel, sizes),
        (
            shape((R, W), F32), shape((R, W), F32), shape((R, R), F32), shape((R, R), F32),
            shape(grad_gate.shape, BF), shape(grad_gate.shape, BF),
        ),
        [
            pltpu.VMEM((2, R, columns), BF), pltpu.VMEM((2, R, columns), BF),
            pltpu.VMEM((2, 512, 128), F32), dma((2,)), dma((2, 2)),
        ],
        "vvvvhh",
        "vvvvhh",
        1 << 27,
        16,
    )(own, theirs, kept, kept_other, grad_gate, grad_up)
    return tuple(outs)


def solution(mesh):
    rows = mesh.shape["row"]
    sizes = (4, 2, 4, 2, 4) if rows == 256 else (2, 2, 2, 2, rows // 16)
    finer = Mesh(mesh.devices.reshape(mesh.shape["outer"], *sizes), ("outer", *ROW))
    return jax.shard_map(
        local,
        mesh=finer,
        in_specs=(P("outer", ROW, None), P("outer", ROW, None), P(None, ROW), P(None, ROW)),
        out_specs=(
            P(None, ROW), P(None, ROW), P(ROW, None), P(ROW, None),
            P("outer", ROW, None), P("outer", ROW, None),
        ),
        check_vma=False,
    )
```

```python
import functools

import jax
import jax.numpy as jnp
from jax import lax
from jax.experimental import pallas as pl
from jax.experimental.pallas import tpu as pltpu
from jax.sharding import Mesh
from jax.sharding import PartitionSpec as P

ROW = ("yq", "yp", "zq", "zp", "x")
NEAR = ("yp", "zp", "x")
FAR = ("yq", "zq")
BF = jnp.bfloat16
F32 = jnp.float32
R = 32
W = 56
BLOCK = 4
TILE = 8
PERIOD = 16 * W
INTERPRET = False


def place(d, sizes):
    _, yp, zq, zp, x = sizes
    at_x, d = d % x, d // x
    at_zp, d = d % zp, d // zp
    at_zq, d = d % zq, d // zq
    at_yp, at_yq = d % yp, d // yp
    near = (at_yp * zp + at_zp) * x + at_x
    return (near * sizes[0] + at_yq) * zq + at_zq


def groups(shape):
    return lax.broadcasted_iota(jnp.int32, shape, 1) // R


def three_terms(x):
    high = x.astype(BF).astype(F32)
    middle = (x - high).astype(BF).astype(F32)
    low = (x - high - middle).astype(BF).astype(F32)
    return high, middle, low


def dot(a, b, ca, cb, precision=None):
    return lax.dot_general(
        a, b, (((ca,), (cb,)), ((), ())), precision=precision, preferred_element_type=F32
    )


def prepare_kernel(bg_ref, bu_ref, gg_ref, gu_ref, block_ref, send_ref, basis, sem):
    core = lax.axis_index("outer")

    @pl.when(core == 0)
    def _():
        pltpu.make_async_copy(bg_ref, basis, sem.at[0]).start()
        pltpu.make_async_copy(gu_ref.at[0], send_ref, sem.at[1]).start()

    @pl.when(core != 0)
    def _():
        pltpu.make_async_copy(bu_ref, basis, sem.at[0]).start()
        pltpu.make_async_copy(gg_ref.at[0], send_ref, sem.at[1]).start()

    pltpu.make_async_copy(bg_ref, basis, sem.at[0]).wait()
    turned = basis[...].astype(F32).T
    empty = jnp.zeros((TILE, R), F32)
    rows = []
    for h in range(2):
        tiles = [turned[8 * t : 8 * t + 8] if t < 7 else empty for t in range(4 * h, 4 * h + 4)]
        rows.append(jnp.concatenate(tiles, axis=1))
    block = jnp.concatenate(rows, axis=0).astype(BF)
    block_ref[...] = jnp.broadcast_to(block[None], block_ref.shape)
    pltpu.make_async_copy(gg_ref.at[0], send_ref, sem.at[1]).wait()


def pack_kernel(sizes, gg_ref, gu_ref, other_ref, packed_ref, turned_ref, own, work, sem):
    core = lax.axis_index("outer")

    @pl.when(core == 0)
    def _():
        pltpu.make_async_copy(gg_ref.at[0], own, sem.at[0]).start()

    @pl.when(core != 0)
    def _():
        pltpu.make_async_copy(gu_ref.at[0], own, sem.at[0]).start()

    pltpu.make_async_copy(gg_ref.at[0], own, sem.at[0]).wait()
    empty = jnp.zeros((TILE, 2 * R), F32)

    @pl.loop(0, packed_ref.shape[0] // 256)
    def _(k):
        columns = pl.ds(pl.multiple_of(k * PERIOD, 128), PERIOD)
        x = jnp.concatenate(
            [own[:, columns].astype(F32), other_ref[:, columns].astype(F32)], axis=0
        )
        xt = x.T
        first = place(16 * k, sizes)
        for d in range(16):
            rows = []
            for h in range(2):
                tiles = []
                for t in range(4 * h, 4 * h + 4):
                    at = 8 * (7 * d + t)
                    tiles.append(xt[at : at + 8] if t < 7 else empty)
                rows.append(jnp.concatenate(tiles, axis=1))
            to = pl.multiple_of(16 * (first + place(d, sizes)), 16)
            work[pl.ds(to, 16), :] = jnp.concatenate(rows, axis=0).astype(BF)

    keep = pltpu.make_async_copy(work, packed_ref, sem.at[1])
    keep.start()

    @pl.loop(0, packed_ref.shape[0] // 256)
    def _(k):
        part = pl.ds(pl.multiple_of(k * 256, 256), 256)
        turned_ref[:, part] = work[part, :].astype(F32).T.astype(BF)

    keep.wait()


def products_kernel(far, basis_ref, turned_ref, packed_ref, sums_ref, left_ref, packed, sem):
    step = 512
    loads = []
    for k in range(packed_ref.shape[0] // step):
        part = pl.ds(k * step, step)
        loads.append(pltpu.make_async_copy(packed_ref.at[part], packed.at[part], sem.at[k]))
        loads[-1].start()
    partial = dot(turned_ref[...], basis_ref[...], 1, 0)
    group = groups((R, 128))
    total = jnp.zeros((R, 128), F32)
    for q in range(4):
        slab = partial[64 * q : 64 * q + R] + partial[64 * q + R : 64 * q + 64]
        total = total + jnp.where(group == q, slab, 0.0)
    total = total + pltpu.roll(total, 64, 1)
    total = total + pltpu.roll(total, 32, 1)
    left = (0.5 * total).astype(BF)
    left_ref[...] = left
    wide = left.astype(F32)
    pieces = []
    for q in range(4):
        one = jnp.where(group == q, wide, 0.0)
        pieces += [one, one]
    spread = jnp.concatenate(pieces, axis=0).astype(BF)
    for load in loads:
        load.wait()
    gram = dot(left, left, 0, 0)[0:R]
    terms = three_terms(jnp.where(group == 3, gram, 0.0))
    row = lax.broadcasted_iota(jnp.int32, (TILE, 128), 0)
    empty = jnp.zeros((TILE, 128), F32)
    extra = []
    for a in range(R // 2):
        tile = empty
        for s in range(6):
            at = 2 * a + s // 3
            tile = jnp.where(row == s, terms[s % 3][at : at + 1], tile)
        extra.append(tile)
    for k in range(len(loads)):
        out = dot(packed[pl.ds(k * step, step), :], spread, 1, 0)
        tiles = []
        for e in range(k * 32, k * 32 + 32):
            tiles += [empty, extra[e // far]]
        sums_ref[pl.ds(k * step, step), :] = (out + jnp.concatenate(tiles, axis=0)).astype(BF)


def summed(parts_ref, scale):
    count, rows, _ = parts_ref.shape

    def add(k, acc):
        return acc + parts_ref[k].astype(F32)

    acc = lax.fori_loop(0, count, add, jnp.zeros((rows, 128), F32), unroll=4)
    acc = acc.reshape(rows // 16, 16, 128)
    row = lax.broadcasted_iota(jnp.int32, acc.shape, 1)
    lane = lax.broadcasted_iota(jnp.int32, acc.shape, 2)
    term = jnp.zeros_like(acc)
    for first in (8, 11):
        gram = acc[:, first : first + 1] + acc[:, first + 1 : first + 2] + acc[:, first + 2 : first + 3]
        for s, part in enumerate(three_terms(gram)):
            term = jnp.where(row == first + s, part, term)
    out = jnp.where((row >= 8) & (lane >= 96), term, scale * acc)
    return out.reshape(rows, 128)


def halfway_kernel(parts_ref, out_ref):
    out_ref[...] = summed(parts_ref, 1.0).astype(BF)


def total_kernel(parts_ref, left_ref, block_ref, kept_ref):
    out = summed(parts_ref, 0.5)
    block_ref[...] = jnp.broadcast_to(out.astype(BF)[None], block_ref.shape)
    kept_ref[0:16] = out
    kept_ref[16:48] = left_ref[...].astype(F32)


def copies_kernel(line_ref, token_ref, out_ref):
    del token_ref
    out_ref[...] = jnp.broadcast_to(line_ref[...][None], out_ref.shape)


def copies_with_gram_kernel(line_ref, kept_other_ref, out_ref):
    line = line_ref[...]
    row = lax.broadcasted_iota(jnp.int32, (16, 128), 0)
    spare = (row >= 8) & (groups((16, 128)) == 3)
    second = jnp.where(spare, kept_other_ref[0:16], line[16:32].astype(F32)).astype(BF)
    line = jnp.concatenate([line[0:16], second, line[32:]], axis=0)
    out_ref[...] = jnp.broadcast_to(line[None], out_ref.shape)


def pick(core, first, second, to, sem, start):
    if not start:
        pltpu.make_async_copy(first, to, sem).wait()
        return

    @pl.when(core == 0)
    def _():
        pltpu.make_async_copy(first, to, sem).start()

    @pl.when(core != 0)
    def _():
        pltpu.make_async_copy(second, to, sem).start()


def residual(sizes, sums_ref, side, grad, resid, gate, up, at, sem):
    pair_group = groups((16, 128))
    second = lax.broadcasted_iota(jnp.int32, (16, 128), 0) >= 8
    masks = []
    for v in range(7):
        a, b = (2 * v) % 7, (2 * v + 1) % 7
        masks.append(jnp.where(pair_group == jnp.where(second, b % 4, a % 4), 1.0, 0.0).astype(BF))
    steps = sums_ref.shape[0] // 256
    cuts = 2
    for cut in range(cuts):

        @pl.loop(cut * steps // cuts, (cut + 1) * steps // cuts)
        def _(k):
            first = place(16 * k, sizes)
            tiles = []
            for d in range(16):
                at_d = pl.multiple_of(16 * (first + place(d, sizes)), 16)
                x = sums_ref[pl.ds(at_d, 16), :]
                tiles += [x[0:8]] * 4 + [x[8:16]] * 3
            rows = []
            for v in range(56):
                pair = jnp.concatenate(tiles[2 * v : 2 * v + 2], axis=0)
                rows.append(pair * masks[v % 7])
            right = jnp.concatenate(rows, axis=0)
            both = dot(side, right, 1, 1)
            columns = pl.ds(pl.multiple_of(k * PERIOD, 128), PERIOD)
            value = grad[:, columns].astype(F32) - (both[0:R] + both[R : 2 * R])
            resid[:, columns] = value.astype(BF)

        part = pl.ds(cut * steps // cuts * PERIOD, steps // cuts * PERIOD)

        @pl.when(at == 0)
        def _():
            pltpu.make_async_copy(resid.at[:, part], gate.at[0, :, part], sem.at[cut]).start()

        @pl.when(at != 0)
        def _():
            pltpu.make_async_copy(resid.at[:, part], up.at[0, :, part], sem.at[cut]).start()

    for cut in range(cuts):
        part = pl.ds(cut * steps // cuts * PERIOD, steps // cuts * PERIOD)
        pltpu.make_async_copy(resid.at[:, part], gate.at[0, :, part], sem.at[cut]).wait()


def solve_kernel(
    sizes, own_ref, kept_ref, kept_other_ref, gg_ref, gu_ref,
    ng_ref, nu_ref, fg_ref, fu_ref, sides_ref, rg_ref, ru_ref,
    grad, resid, tiles, grams, sem_in, sem_out,
):
    core = lax.axis_index("outer")
    pick(core, gg_ref.at[0], gu_ref.at[0], grad, sem_in, True)
    far = sizes[0] * sizes[2]
    high = lax.Precision.HIGHEST
    group = groups((R, 128))
    row = lax.broadcasted_iota(jnp.int32, (R, 128), 0)
    lane = lax.broadcasted_iota(jnp.int32, (R, 128), 1)
    half = R // 2
    for j in range(2):
        for a in range(half):
            at = 16 * (far * a + j)
            tiles[j, 8 * a : 8 * a + 8] = own_ref[at : at + 16].astype(F32)[8:16]
        for odd in range(2):
            gram = tiles.at[j][pl.ds(3 * odd, half, stride=8), :]
            for s in range(1, 3):
                gram = gram + tiles.at[j][pl.ds(3 * odd + s, half, stride=8), :]
            grams.at[j][pl.ds(odd, half, stride=2), :] = gram
    own_gram = pltpu.roll(grams[0], 32, 1)
    other_gram = pltpu.roll(grams[1], 96, 1)
    m = jnp.where(group == 0, own_gram, jnp.where(group == 2, other_gram, 0.0))
    m = jnp.where((group % 2 == 1) & (row == lane % R), 1.0, m)
    pivots = jnp.ones((R, 128), F32)
    for first in range(0, R, BLOCK):
        columns = []
        for k in range(first, first + BLOCK):
            left = jnp.broadcast_to(m[:, k : k + 1], (R, 128))
            right = jnp.broadcast_to(m[:, 64 + k : 65 + k], (R, 128))
            columns.append(jnp.where(lane < 64, left, right))
        rows = [m[k : k + 1] for k in range(first, first + BLOCK)]
        for i in range(BLOCK):
            k = first + i
            pivot = columns[i][k : k + 1]
            pivots = jnp.where(row == k, pivot, pivots)
            factor = jnp.where(row > k, columns[i] * (1.0 / pivot), 0.0)
            for j in range(i + 1, BLOCK):
                columns[j] = columns[j] - factor * columns[j][k : k + 1]
                at = first + j
                rows[j] = rows[j] - factor[at : at + 1] * rows[i]
            m = m - factor * rows[i]
    scale = lax.rsqrt(pivots)
    scale = scale * (1.5 - 0.5 * pivots * scale * scale)
    inverse = m * scale
    kept = (kept_ref[...], kept_other_ref[...])
    nexts, factors = [], []
    for j in range(2):
        at = 1 if j == 0 else 3
        one = jnp.where(group == at, inverse, 0.0)
        one = one + pltpu.roll(one, 64, 1)
        one = one + pltpu.roll(one, 32, 1)
        u = kept[j][0:16]
        left = kept[j][16:48]
        rows = []
        for t in range(7):
            h, q = divmod(t, 4)
            rows.append(jnp.where(groups((TILE, 128)) == q, u[8 * h : 8 * h + 8], 0.0))
        nexts.append(dot(one, jnp.concatenate(rows, axis=0), 1, 1, high))
        factor = dot(jnp.where(group == 0, left, 0.0), one, 1, 1, high)
        factors.append(factor)
        side = dot(factor, one, 1, 0, high)
        top = side.astype(BF)
        rest = (side - top.astype(F32)).astype(BF)
        sides_ref[j, 0:R] = top
        sides_ref[j, R : 2 * R] = rest
    swap = core != 0
    ng_ref[...] = jnp.where(swap, nexts[1], nexts[0])
    nu_ref[...] = jnp.where(swap, nexts[0], nexts[1])
    fg_ref[...] = jnp.where(swap, factors[1], factors[0])
    fu_ref[...] = jnp.where(swap, factors[0], factors[1])
    pick(core, gg_ref.at[0], gu_ref.at[0], grad, sem_in, False)
    residual(sizes, own_ref, sides_ref[0], grad, resid, rg_ref, ru_ref, core, sem_out)


def other_kernel(
    sizes, sums_ref, sides_ref, gg_ref, gu_ref, rg_in, ru_in, rg_ref, ru_ref,
    grad, resid, sem_in, sem_out,
):
    del rg_in, ru_in
    core = lax.axis_index("outer")
    pick(core, gu_ref.at[0], gg_ref.at[0], grad, sem_in, True)
    pick(core, gu_ref.at[0], gg_ref.at[0], grad, sem_in, False)
    residual(sizes, sums_ref, sides_ref[1], grad, resid, rg_ref, ru_ref, 1 - core, sem_out)


def call(kernel, outs, scratch, spaces_in, spaces_out, cost, limit, aliases={}):
    space = {"h": pltpu.HBM, "v": pltpu.VMEM}
    specs_out = tuple(pl.BlockSpec(memory_space=space[s]) for s in spaces_out)
    run = pl.pallas_call(
        kernel,
        out_shape=[
            pltpu.HBM(o.shape, o.dtype) if s == "h" and not INTERPRET else o
            for s, o in zip(spaces_out, outs)
        ],
        in_specs=[pl.BlockSpec(memory_space=space[s]) for s in spaces_in],
        out_specs=specs_out,
        scratch_shapes=scratch,
        input_output_aliases=aliases,
        cost_estimate=pl.CostEstimate(flops=cost, bytes_accessed=cost // 16, transcendentals=0),
        compiler_params=pltpu.CompilerParams(vmem_limit_bytes=limit << 20),
        interpret=INTERPRET,
    )

    def pinned(*args):
        return run(
            *(
                pltpu.with_memory_space_constraint(x, pltpu.HBM) if s == "h" and not INTERPRET else x
                for s, x in zip(spaces_in, args)
            )
        )

    return pinned


def shape(dims, dtype):
    return jax.ShapeDtypeStruct(dims, dtype)


def local(grad_gate, grad_up, basis_gate, basis_up):
    sizes = tuple(lax.axis_size(a) for a in ROW)
    near, far = lax.axis_size(NEAR), lax.axis_size(FAR)
    columns = grad_gate.shape[2]
    packed_rows = 16 * near * far
    swap = [(0, 1), (1, 0)]
    dma = pltpu.SemaphoreType.DMA

    def exchange(x, axes):
        return lax.all_to_all(x, axes, 0, 0, tiled=True)

    def gather(block, kernel, other):
        line = exchange(block, FAR).reshape(16 * far, 128)
        outs = (shape((near, 16 * far, 128), BF),)
        space = "h" if other.dtype == BF else "v"
        (copies,) = call(kernel, outs, [], "v" + space, "v", 1 << 20, 4)(line, other)
        return exchange(copies, NEAR).reshape(packed_rows, 128)

    block, send = call(
        prepare_kernel,
        (shape((far, 16, 128), BF), shape((R, columns), BF)),
        [pltpu.VMEM((R, W), BF), dma((2,))],
        "hhhh",
        "vv",
        1 << 20,
        6,
    )(basis_gate, basis_up, grad_gate, grad_up)
    other = lax.ppermute(send, "outer", swap)
    packed, turned = call(
        functools.partial(pack_kernel, sizes),
        (shape((packed_rows, 256), BF), shape((256, packed_rows), BF)),
        [pltpu.VMEM((R, columns), BF), pltpu.VMEM((packed_rows, 256), BF), dma((2,))],
        "hhv",
        "hv",
        1 << 26,
        16,
    )(grad_gate, grad_up, other)
    basis = gather(block, copies_kernel, packed)
    sums, left = call(
        functools.partial(products_kernel, far),
        (shape((packed_rows, 128), BF), shape((R, 128), BF)),
        [pltpu.VMEM((packed_rows, 256), BF), dma((packed_rows // 512,))],
        "vvh",
        "vv",
        1 << 26,
        16,
    )(basis, turned, packed)
    parts = exchange(sums.reshape(near, 16 * far, 128), NEAR)
    (halfway,) = call(halfway_kernel, (shape((16 * far, 128), BF),), [], "v", "v", 1 << 20, 8)(parts)
    parts = exchange(halfway.reshape(far, 16, 128), FAR)
    block, kept = call(
        total_kernel,
        (shape((far, 16, 128), BF), shape((48, 128), F32)),
        [],
        "vv",
        "vv",
        1 << 20,
        4,
    )(parts, left)
    kept_other = lax.ppermute(kept, "outer", swap)
    own = gather(block, copies_with_gram_kernel, kept_other)
    theirs = lax.ppermute(own, "outer", swap)
    working = [pltpu.VMEM((R, columns), BF), pltpu.VMEM((R, columns), BF)]
    resids = (shape(grad_gate.shape, BF), shape(grad_gate.shape, BF))
    *small, sides, rg, ru = call(
        functools.partial(solve_kernel, sizes),
        (
            shape((R, W), F32), shape((R, W), F32), shape((R, R), F32), shape((R, R), F32),
            shape((2, 2 * R, 128), BF), *resids,
        ),
        [*working, pltpu.VMEM((2, 128, 128), F32), pltpu.VMEM((2, R, 128), F32), dma, dma((2,))],
        "vvvhh",
        "vvvvvhh",
        1 << 27,
        12,
    )(own, kept, kept_other, grad_gate, grad_up)
    rg, ru = call(
        functools.partial(other_kernel, sizes),
        resids,
        [*working, dma, dma((2,))],
        "vvhhhh",
        "hh",
        1 << 26,
        12,
        {4: 0, 5: 1},
    )(theirs, sides, grad_gate, grad_up, rg, ru)
    return (*small, rg, ru)


def solution(mesh):
    rows = mesh.shape["row"]
    sizes = (4, 2, 4, 2, 4) if rows == 256 else (2, 2, 1, 2, rows // 8)
    finer = Mesh(mesh.devices.reshape(mesh.shape["outer"], *sizes), ("outer", *ROW))
    return jax.shard_map(
        local,
        mesh=finer,
        in_specs=(P("outer", ROW, None), P("outer", ROW, None), P(None, ROW), P(None, ROW)),
        out_specs=(
            P(None, ROW), P(None, ROW), P(ROW, None), P(ROW, None),
            P("outer", ROW, None), P("outer", ROW, None),
        ),
        check_vma=False,
    )
```

```python
import functools

import jax
import jax.numpy as jnp
from jax import lax
from jax.experimental import pallas as pl
from jax.experimental.pallas import tpu as pltpu
from jax.sharding import Mesh
from jax.sharding import PartitionSpec as P

ROW = ("yq", "yp", "zq", "zp", "x")
NEAR = ("yp", "zp", "x")
FAR = ("yq", "zq")
BF = jnp.bfloat16
F32 = jnp.float32
R = 32
W = 56
BLOCK = 4
TILE = 8
PERIOD = 16 * W
INTERPRET = False


def place(d, sizes):
    _, yp, zq, zp, x = sizes
    at_x, d = d % x, d // x
    at_zp, d = d % zp, d // zp
    at_zq, d = d % zq, d // zq
    at_yp, at_yq = d % yp, d // yp
    near = (at_yp * zp + at_zp) * x + at_x
    return (near * sizes[0] + at_yq) * zq + at_zq


def groups(shape):
    return lax.broadcasted_iota(jnp.int32, shape, 1) // R


def three_terms(x):
    high = x.astype(BF).astype(F32)
    middle = (x - high).astype(BF).astype(F32)
    low = (x - high - middle).astype(BF).astype(F32)
    return high, middle, low


def dot(a, b, ca, cb, precision=None):
    return lax.dot_general(
        a, b, (((ca,), (cb,)), ((), ())), precision=precision, preferred_element_type=F32
    )


def prepare_kernel(bg_ref, bu_ref, gg_ref, gu_ref, block_ref, send_ref, basis, sem):
    core = lax.axis_index("outer")

    @pl.when(core == 0)
    def _():
        pltpu.make_async_copy(bg_ref, basis, sem.at[0]).start()
        pltpu.make_async_copy(gu_ref.at[0], send_ref, sem.at[1]).start()

    @pl.when(core != 0)
    def _():
        pltpu.make_async_copy(bu_ref, basis, sem.at[0]).start()
        pltpu.make_async_copy(gg_ref.at[0], send_ref, sem.at[1]).start()

    pltpu.make_async_copy(bg_ref, basis, sem.at[0]).wait()
    turned = basis[...].astype(F32).T
    empty = jnp.zeros((TILE, R), F32)
    rows = []
    for h in range(2):
        tiles = [turned[8 * t : 8 * t + 8] if t < 7 else empty for t in range(4 * h, 4 * h + 4)]
        rows.append(jnp.concatenate(tiles, axis=1))
    block = jnp.concatenate(rows, axis=0).astype(BF)
    block_ref[...] = jnp.broadcast_to(block[None], block_ref.shape)
    pltpu.make_async_copy(gg_ref.at[0], send_ref, sem.at[1]).wait()


def pack_kernel(sizes, gg_ref, gu_ref, other_ref, packed_ref, turned_ref, own, work, sem):
    core = lax.axis_index("outer")

    @pl.when(core == 0)
    def _():
        pltpu.make_async_copy(gg_ref.at[0], own, sem.at[0]).start()

    @pl.when(core != 0)
    def _():
        pltpu.make_async_copy(gu_ref.at[0], own, sem.at[0]).start()

    pltpu.make_async_copy(gg_ref.at[0], own, sem.at[0]).wait()
    empty = jnp.zeros((TILE, 2 * R), F32)

    @pl.loop(0, packed_ref.shape[0] // 256)
    def _(k):
        columns = pl.ds(pl.multiple_of(k * PERIOD, 128), PERIOD)
        x = jnp.concatenate(
            [own[:, columns].astype(F32), other_ref[:, columns].astype(F32)], axis=0
        )
        xt = x.T
        first = place(16 * k, sizes)
        for d in range(16):
            rows = []
            for h in range(2):
                tiles = []
                for t in range(4 * h, 4 * h + 4):
                    at = 8 * (7 * d + t)
                    tiles.append(xt[at : at + 8] if t < 7 else empty)
                rows.append(jnp.concatenate(tiles, axis=1))
            to = pl.multiple_of(16 * (first + place(d, sizes)), 16)
            work[pl.ds(to, 16), :] = jnp.concatenate(rows, axis=0).astype(BF)

    keep = pltpu.make_async_copy(work, packed_ref, sem.at[1])
    keep.start()

    @pl.loop(0, packed_ref.shape[0] // 256)
    def _(k):
        part = pl.ds(pl.multiple_of(k * 256, 256), 256)
        turned_ref[:, part] = work[part, :].astype(F32).T.astype(BF)

    keep.wait()


def products_kernel(far, basis_ref, turned_ref, packed_ref, sums_ref, left_ref, packed, sem):
    step = 512
    loads = []
    for k in range(packed_ref.shape[0] // step):
        part = pl.ds(k * step, step)
        loads.append(pltpu.make_async_copy(packed_ref.at[part], packed.at[part], sem.at[k]))
        loads[-1].start()
    partial = dot(turned_ref[...], basis_ref[...], 1, 0)
    group = groups((R, 128))
    total = jnp.zeros((R, 128), F32)
    for q in range(4):
        slab = partial[64 * q : 64 * q + R] + partial[64 * q + R : 64 * q + 64]
        total = total + jnp.where(group == q, slab, 0.0)
    total = total + pltpu.roll(total, 64, 1)
    total = total + pltpu.roll(total, 32, 1)
    left = (0.5 * total).astype(BF)
    left_ref[...] = left
    wide = left.astype(F32)
    pieces = []
    for q in range(4):
        one = jnp.where(group == q, wide, 0.0)
        pieces += [one, one]
    spread = jnp.concatenate(pieces, axis=0).astype(BF)
    for load in loads:
        load.wait()
    gram = dot(left, left, 0, 0)[0:R]
    terms = three_terms(jnp.where(group == 3, gram, 0.0))
    row = lax.broadcasted_iota(jnp.int32, (TILE, 128), 0)
    empty = jnp.zeros((TILE, 128), F32)
    extra = []
    for a in range(R // 2):
        tile = empty
        for s in range(6):
            at = 2 * a + s // 3
            tile = jnp.where(row == s, terms[s % 3][at : at + 1], tile)
        extra.append(tile)
    tiles = []
    for e in range(step // 16):
        tiles += [empty, extra[e % far]]
    added = jnp.concatenate(tiles, axis=0)
    for k in range(len(loads)):
        out = dot(packed[pl.ds(k * step, step), :], spread, 1, 0)
        sums_ref[pl.ds(k * step, step), :] = (out + added).astype(BF)


def summed(parts_ref, scale):
    count, rows, _ = parts_ref.shape

    def add(k, acc):
        return acc + parts_ref[k].astype(F32)

    acc = lax.fori_loop(0, count, add, jnp.zeros((rows, 128), F32), unroll=4)
    acc = acc.reshape(rows // 16, 16, 128)
    row = lax.broadcasted_iota(jnp.int32, acc.shape, 1)
    lane = lax.broadcasted_iota(jnp.int32, acc.shape, 2)
    term = jnp.zeros_like(acc)
    for first in (8, 11):
        gram = acc[:, first : first + 1] + acc[:, first + 1 : first + 2] + acc[:, first + 2 : first + 3]
        for s, part in enumerate(three_terms(gram)):
            term = jnp.where(row == first + s, part, term)
    out = jnp.where((row >= 8) & (lane >= 96), term, scale * acc)
    return out.reshape(rows, 128)


def halfway_kernel(parts_ref, out_ref):
    out_ref[...] = summed(parts_ref, 1.0).astype(BF)


def total_kernel(parts_ref, block_ref, kept_ref):
    out = summed(parts_ref, 0.5)
    block_ref[...] = jnp.broadcast_to(out.astype(BF)[None], block_ref.shape)
    kept_ref[...] = out


def pick(core, first, second, to, sem, start):
    if not start:
        pltpu.make_async_copy(first, to, sem).wait()
        return

    @pl.when(core == 0)
    def _():
        pltpu.make_async_copy(first, to, sem).start()

    @pl.when(core != 0)
    def _():
        pltpu.make_async_copy(second, to, sem).start()


def solve_kernel(line_ref, kept_ref, left_ref, out_ref, tiles, grams):
    high = lax.Precision.HIGHEST
    group = groups((R, 128))
    row = lax.broadcasted_iota(jnp.int32, (R, 128), 0)
    lane = lax.broadcasted_iota(jnp.int32, (R, 128), 1)
    half = R // 2
    for f in range(half):
        tiles[8 * f : 8 * f + 8] = line_ref[16 * f : 16 * f + 16].astype(F32)[8:16]
    for odd in range(2):
        gram = tiles[pl.ds(3 * odd, half, stride=8), :]
        for s in range(1, 3):
            gram = gram + tiles[pl.ds(3 * odd + s, half, stride=8), :]
        grams[pl.ds(odd, half, stride=2), :] = gram
    m = jnp.where(group == 0, pltpu.roll(grams[...], 32, 1), 0.0)
    m = jnp.where((group == 1) & (row == lane % R), 1.0, m)
    pivots = jnp.ones((R, 128), F32)
    for first in range(0, R, BLOCK):
        columns = [jnp.broadcast_to(m[:, k : k + 1], (R, 128)) for k in range(first, first + BLOCK)]
        rows = [m[k : k + 1] for k in range(first, first + BLOCK)]
        for i in range(BLOCK):
            k = first + i
            pivot = columns[i][k : k + 1]
            pivots = jnp.where(row == k, pivot, pivots)
            factor = jnp.where(row > k, columns[i] * (1.0 / pivot), 0.0)
            for j in range(i + 1, BLOCK):
                columns[j] = columns[j] - factor * columns[j][k : k + 1]
                at = first + j
                rows[j] = rows[j] - factor[at : at + 1] * rows[i]
            m = m - factor * rows[i]
    scale = lax.rsqrt(pivots)
    scale = scale * (1.5 - 0.5 * pivots * scale * scale)
    one = jnp.where(group == 1, m * scale, 0.0)
    one = one + pltpu.roll(one, 64, 1)
    one = one + pltpu.roll(one, 32, 1)
    u = kept_ref[...]
    rows = []
    for t in range(7):
        h, q = divmod(t, 4)
        rows.append(jnp.where(groups((TILE, 128)) == q, u[8 * h : 8 * h + 8], 0.0))
    rows.append(jnp.zeros((128 - W, 128), F32))
    nexts = dot(one, jnp.concatenate(rows, axis=0), 1, 1, high)
    left = jnp.where(group == 0, left_ref[...].astype(F32), 0.0)
    tall = jnp.concatenate([one, one, one, one], axis=0)
    factors = dot(left, tall, 1, 1, high)
    out_ref[0:R] = jnp.where(lane < 64, nexts, factors)
    out_ref[R : 2 * R] = dot(factors[:, 0:R], one, 1, 0, high)


CUTS = 4


def residual(sizes, sums_ref, side, grad, resid, gate, up, at, sem):
    top = side.astype(BF)
    rest = (side - top.astype(F32)).astype(BF)
    side = jnp.concatenate([top, rest], axis=0)
    pair_group = groups((16, 128))
    second = lax.broadcasted_iota(jnp.int32, (16, 128), 0) >= 8
    masks = []
    for v in range(7):
        a, b = (2 * v) % 7, (2 * v + 1) % 7
        masks.append(jnp.where(pair_group == jnp.where(second, b % 4, a % 4), 1.0, 0.0).astype(BF))
    steps = sums_ref.shape[0] // 256
    cuts = min(CUTS, steps)
    parts = [pl.ds(c * steps // cuts * PERIOD, steps // cuts * PERIOD) for c in range(cuts)]
    for cut, part in enumerate(parts):

        @pl.loop(cut * steps // cuts, (cut + 1) * steps // cuts)
        def _(k):
            first = place(16 * k, sizes)
            tiles = []
            for d in range(16):
                at_d = pl.multiple_of(16 * (first + place(d, sizes)), 16)
                x = sums_ref[pl.ds(at_d, 16), :]
                tiles += [x[0:8]] * 4 + [x[8:16]] * 3
            rows = []
            for v in range(56):
                pair = jnp.concatenate(tiles[2 * v : 2 * v + 2], axis=0)
                rows.append(pair * masks[v % 7])
            right = jnp.concatenate(rows, axis=0)
            both = dot(side, right, 1, 1)
            columns = pl.ds(pl.multiple_of(k * PERIOD, 128), PERIOD)
            value = grad[:, columns].astype(F32) - (both[0:R] + both[R : 2 * R])
            resid[:, columns] = value.astype(BF)

        @pl.when(at == 0)
        def _():
            pltpu.make_async_copy(resid.at[:, part], gate.at[0, :, part], sem.at[cut]).start()

        @pl.when(at != 0)
        def _():
            pltpu.make_async_copy(resid.at[:, part], up.at[0, :, part], sem.at[cut]).start()

    for cut, part in enumerate(parts):
        pltpu.make_async_copy(resid.at[:, part], gate.at[0, :, part], sem.at[cut]).wait()


def own_kernel(
    sizes, sums_ref, own_ref, other_ref, gg_ref, gu_ref,
    ng_ref, nu_ref, fg_ref, fu_ref, other_grad_ref, rg_ref, ru_ref,
    grad, resid, sem_in, sem_out,
):
    core = lax.axis_index("outer")
    pick(core, gg_ref.at[0], gu_ref.at[0], grad, sem_in.at[0], True)
    pick(core, gu_ref.at[0], gg_ref.at[0], other_grad_ref, sem_in.at[1], True)
    own, other = own_ref[0:R], other_ref[0:R]
    gate, up = jnp.where(core == 0, own, other), jnp.where(core == 0, other, own)
    ng_ref[...] = gate[:, 0:W]
    nu_ref[...] = up[:, 0:W]
    fg_ref[...] = gate[:, 64 : 64 + R]
    fu_ref[...] = up[:, 64 : 64 + R]
    pick(core, gg_ref.at[0], gu_ref.at[0], grad, sem_in.at[0], False)
    residual(sizes, sums_ref, own_ref[R : 2 * R], grad, resid, rg_ref, ru_ref, core, sem_out)
    pick(core, gu_ref.at[0], gg_ref.at[0], other_grad_ref, sem_in.at[1], False)


def other_kernel(sizes, sums_ref, other_ref, grad, rg_in, ru_in, rg_ref, ru_ref, resid, sem_out):
    del rg_in, ru_in
    core = lax.axis_index("outer")
    residual(sizes, sums_ref, other_ref[R : 2 * R], grad, resid, rg_ref, ru_ref, 1 - core, sem_out)


def call(kernel, outs, scratch, spaces_in, spaces_out, cost, limit, aliases={}):
    space = {"h": pltpu.HBM, "v": pltpu.VMEM}
    specs_out = tuple(pl.BlockSpec(memory_space=space[s]) for s in spaces_out)
    run = pl.pallas_call(
        kernel,
        out_shape=[
            pltpu.HBM(o.shape, o.dtype) if s == "h" and not INTERPRET else o
            for s, o in zip(spaces_out, outs)
        ],
        in_specs=[pl.BlockSpec(memory_space=space[s]) for s in spaces_in],
        out_specs=specs_out,
        scratch_shapes=scratch,
        input_output_aliases=aliases,
        cost_estimate=pl.CostEstimate(flops=cost, bytes_accessed=cost // 16, transcendentals=0),
        compiler_params=pltpu.CompilerParams(vmem_limit_bytes=limit << 20),
        interpret=INTERPRET,
    )

    def pinned(*args):
        return run(
            *(
                pltpu.with_memory_space_constraint(x, pltpu.HBM) if s == "h" and not INTERPRET else x
                for s, x in zip(spaces_in, args)
            )
        )

    return pinned


def shape(dims, dtype):
    return jax.ShapeDtypeStruct(dims, dtype)


def local(grad_gate, grad_up, basis_gate, basis_up):
    sizes = tuple(lax.axis_size(a) for a in ROW)
    near, far = lax.axis_size(NEAR), lax.axis_size(FAR)
    columns = grad_gate.shape[2]
    packed_rows = 16 * near * far
    swap = [(0, 1), (1, 0)]
    dma = pltpu.SemaphoreType.DMA

    def exchange(x, axes):
        return lax.all_to_all(x, axes, 0, 0, tiled=True)

    def gather_far(block):
        return exchange(block, FAR).reshape(16 * far, 128)

    def gather_near(line):
        copies = jnp.broadcast_to(line[None], (near, 16 * far, 128))
        return exchange(copies, NEAR).reshape(packed_rows, 128)

    block, send = call(
        prepare_kernel,
        (shape((far, 16, 128), BF), shape((R, columns), BF)),
        [pltpu.VMEM((R, W), BF), dma((2,))],
        "hhhh",
        "vv",
        1 << 20,
        6,
    )(basis_gate, basis_up, grad_gate, grad_up)
    other = lax.ppermute(send, "outer", swap)
    packed, turned = call(
        functools.partial(pack_kernel, sizes),
        (shape((packed_rows, 256), BF), shape((256, packed_rows), BF)),
        [pltpu.VMEM((R, columns), BF), pltpu.VMEM((packed_rows, 256), BF), dma((2,))],
        "hhv",
        "hv",
        1 << 26,
        16,
    )(grad_gate, grad_up, other)
    basis = gather_near(gather_far(block))
    sums, left = call(
        functools.partial(products_kernel, far),
        (shape((packed_rows, 128), BF), shape((R, 128), BF)),
        [pltpu.VMEM((packed_rows, 256), BF), dma((packed_rows // 512,))],
        "vvh",
        "vv",
        1 << 26,
        16,
    )(basis, turned, packed)
    parts = exchange(sums.reshape(near, 16 * far, 128), NEAR)
    (halfway,) = call(halfway_kernel, (shape((16 * far, 128), BF),), [], "v", "v", 1 << 20, 8)(parts)
    parts = exchange(halfway.reshape(far, 16, 128), FAR)
    block, kept = call(
        total_kernel,
        (shape((far, 16, 128), BF), shape((16, 128), F32)),
        [],
        "v",
        "vv",
        1 << 20,
        4,
    )(parts)
    line = gather_far(block)
    (own,) = call(
        solve_kernel,
        (shape((2 * R, 128), F32),),
        [pltpu.VMEM((128, 128), F32), pltpu.VMEM((R, 128), F32)],
        "vvv",
        "v",
        1 << 26,
        4,
    )(line, kept, left)
    other = lax.ppermute(own, "outer", swap)
    sums, other = lax.optimization_barrier((gather_near(line), other))
    sums_other = lax.ppermute(sums, "outer", swap)
    working = pltpu.VMEM((R, columns), BF)
    resids = (shape(grad_gate.shape, BF), shape(grad_gate.shape, BF))
    *small, other_grad, rg, ru = call(
        functools.partial(own_kernel, sizes),
        (
            shape((R, W), F32), shape((R, W), F32), shape((R, R), F32), shape((R, R), F32),
            shape((R, columns), BF), *resids,
        ),
        [working, working, dma((2,)), dma((CUTS,))],
        "vvvhh",
        "vvvvvhh",
        1 << 26,
        12,
    )(sums, own, other, grad_gate, grad_up)
    rg, ru = call(
        functools.partial(other_kernel, sizes),
        resids,
        [working, dma((CUTS,))],
        "vvvhh",
        "hh",
        1 << 26,
        12,
        {3: 0, 4: 1},
    )(sums_other, other, other_grad, rg, ru)
    return (*small, rg, ru)


def solution(mesh):
    rows = mesh.shape["row"]
    sizes = (4, 2, 4, 2, 4) if rows == 256 else (4, 1, 4, 1, rows // 16)
    finer = Mesh(mesh.devices.reshape(mesh.shape["outer"], *sizes), ("outer", *ROW))
    return jax.shard_map(
        local,
        mesh=finer,
        in_specs=(P("outer", ROW, None), P("outer", ROW, None), P(None, ROW), P(None, ROW)),
        out_specs=(
            P(None, ROW), P(None, ROW), P(ROW, None), P(ROW, None),
            P("outer", ROW, None), P("outer", ROW, None),
        ),
        check_vma=False,
    )
```

```python
import functools

import jax
import jax.numpy as jnp
from jax import lax
from jax.experimental import pallas as pl
from jax.experimental.pallas import tpu as pltpu
from jax.sharding import Mesh
from jax.sharding import PartitionSpec as P

ROW = ("yq", "yp", "zq", "zp", "x")
NEAR = ("yp", "zp", "x")
FAR = ("yq", "zq")
BF = jnp.bfloat16
F32 = jnp.float32
R = 32
W = 56
BLOCK = 4
TILE = 8
PERIOD = 16 * W
INTERPRET = False


def place(d, sizes):
    _, yp, zq, zp, x = sizes
    at_x, d = d % x, d // x
    at_zp, d = d % zp, d // zp
    at_zq, d = d % zq, d // zq
    at_yp, at_yq = d % yp, d // yp
    near = (at_yp * zp + at_zp) * x + at_x
    return (near * sizes[0] + at_yq) * zq + at_zq


def groups(shape):
    return lax.broadcasted_iota(jnp.int32, shape, 1) // R


def three_terms(x):
    high = x.astype(BF).astype(F32)
    middle = (x - high).astype(BF).astype(F32)
    low = (x - high - middle).astype(BF).astype(F32)
    return high, middle, low


def dot(a, b, ca, cb, precision=None):
    return lax.dot_general(
        a, b, (((ca,), (cb,)), ((), ())), precision=precision, preferred_element_type=F32
    )


def prepare_kernel(bg_ref, bu_ref, gg_ref, gu_ref, block_ref, send_ref, basis, sem):
    core = lax.axis_index("outer")

    @pl.when(core == 0)
    def _():
        pltpu.make_async_copy(bg_ref, basis, sem.at[0]).start()
        pltpu.make_async_copy(gu_ref.at[0], send_ref, sem.at[1]).start()

    @pl.when(core != 0)
    def _():
        pltpu.make_async_copy(bu_ref, basis, sem.at[0]).start()
        pltpu.make_async_copy(gg_ref.at[0], send_ref, sem.at[1]).start()

    pltpu.make_async_copy(bg_ref, basis, sem.at[0]).wait()
    turned = basis[...].astype(F32).T
    empty = jnp.zeros((TILE, R), F32)
    rows = []
    for h in range(2):
        tiles = [turned[8 * t : 8 * t + 8] if t < 7 else empty for t in range(4 * h, 4 * h + 4)]
        rows.append(jnp.concatenate(tiles, axis=1))
    block = jnp.concatenate(rows, axis=0).astype(BF)
    block_ref[...] = jnp.broadcast_to(block[None], block_ref.shape)
    pltpu.make_async_copy(gg_ref.at[0], send_ref, sem.at[1]).wait()


def pack_kernel(sizes, gg_ref, gu_ref, other_ref, packed_ref, turned_ref, own, work, sem):
    core = lax.axis_index("outer")

    @pl.when(core == 0)
    def _():
        pltpu.make_async_copy(gg_ref.at[0], own, sem.at[0]).start()

    @pl.when(core != 0)
    def _():
        pltpu.make_async_copy(gu_ref.at[0], own, sem.at[0]).start()

    pltpu.make_async_copy(gg_ref.at[0], own, sem.at[0]).wait()
    empty = jnp.zeros((TILE, 2 * R), F32)

    @pl.loop(0, packed_ref.shape[0] // 256)
    def _(k):
        columns = pl.ds(pl.multiple_of(k * PERIOD, 128), PERIOD)
        x = jnp.concatenate(
            [own[:, columns].astype(F32), other_ref[:, columns].astype(F32)], axis=0
        )
        xt = x.T
        first = place(16 * k, sizes)
        for d in range(16):
            rows = []
            for h in range(2):
                tiles = []
                for t in range(4 * h, 4 * h + 4):
                    at = 8 * (7 * d + t)
                    tiles.append(xt[at : at + 8] if t < 7 else empty)
                rows.append(jnp.concatenate(tiles, axis=1))
            to = pl.multiple_of(16 * (first + place(d, sizes)), 16)
            work[pl.ds(to, 16), :] = jnp.concatenate(rows, axis=0).astype(BF)

    keep = pltpu.make_async_copy(work, packed_ref, sem.at[1])
    keep.start()

    @pl.loop(0, packed_ref.shape[0] // 256)
    def _(k):
        part = pl.ds(pl.multiple_of(k * 256, 256), 256)
        turned_ref[:, part] = work[part, :].astype(F32).T.astype(BF)

    keep.wait()


def products_kernel(far, basis_ref, turned_ref, packed_ref, sums_ref, left_ref, packed, sem):
    step = 512
    loads = []
    for k in range(packed_ref.shape[0] // step):
        part = pl.ds(k * step, step)
        loads.append(pltpu.make_async_copy(packed_ref.at[part], packed.at[part], sem.at[k]))
        loads[-1].start()
    partial = dot(turned_ref[...], basis_ref[...], 1, 0)
    group = groups((R, 128))
    total = jnp.zeros((R, 128), F32)
    for q in range(4):
        slab = partial[64 * q : 64 * q + R] + partial[64 * q + R : 64 * q + 64]
        total = total + jnp.where(group == q, slab, 0.0)
    total = total + pltpu.roll(total, 64, 1)
    total = total + pltpu.roll(total, 32, 1)
    left = (0.5 * total).astype(BF)
    left_ref[...] = left
    wide = left.astype(F32)
    pieces = []
    for q in range(4):
        one = jnp.where(group == q, wide, 0.0)
        pieces += [one, one]
    spread = jnp.concatenate(pieces, axis=0).astype(BF)
    for load in loads:
        load.wait()
    gram = dot(left, left, 0, 0)[0:R]
    terms = three_terms(jnp.where(group == 3, gram, 0.0))
    row = lax.broadcasted_iota(jnp.int32, (TILE, 128), 0)
    empty = jnp.zeros((TILE, 128), F32)
    extra = []
    for a in range(R // 2):
        tile = empty
        for s in range(6):
            at = 2 * a + s // 3
            tile = jnp.where(row == s, terms[s % 3][at : at + 1], tile)
        extra.append(tile)
    tiles = []
    for e in range(step // 16):
        tiles += [empty, extra[e % far]]
    added = jnp.concatenate(tiles, axis=0)
    for k in range(len(loads)):
        out = dot(packed[pl.ds(k * step, step), :], spread, 1, 0)
        sums_ref[pl.ds(k * step, step), :] = (out + added).astype(BF)


def summed(parts_ref, scale):
    count, rows, _ = parts_ref.shape

    def add(k, acc):
        return acc + parts_ref[k].astype(F32)

    acc = lax.fori_loop(0, count, add, jnp.zeros((rows, 128), F32), unroll=4)
    acc = acc.reshape(rows // 16, 16, 128)
    row = lax.broadcasted_iota(jnp.int32, acc.shape, 1)
    lane = lax.broadcasted_iota(jnp.int32, acc.shape, 2)
    term = jnp.zeros_like(acc)
    for first in (8, 11):
        gram = acc[:, first : first + 1] + acc[:, first + 1 : first + 2] + acc[:, first + 2 : first + 3]
        for s, part in enumerate(three_terms(gram)):
            term = jnp.where(row == first + s, part, term)
    out = jnp.where((row >= 8) & (lane >= 96), term, scale * acc)
    return out.reshape(rows, 128)


def halfway_kernel(parts_ref, out_ref):
    out_ref[...] = summed(parts_ref, 1.0).astype(BF)


def total_kernel(parts_ref, block_ref, kept_ref):
    out = summed(parts_ref, 0.5)
    block_ref[...] = jnp.broadcast_to(out.astype(BF)[None], block_ref.shape)
    kept_ref[...] = out


def pick(core, first, second, to, sem, start):
    if not start:
        pltpu.make_async_copy(first, to, sem).wait()
        return

    @pl.when(core == 0)
    def _():
        pltpu.make_async_copy(first, to, sem).start()

    @pl.when(core != 0)
    def _():
        pltpu.make_async_copy(second, to, sem).start()


def solve_kernel(
    line_ref, kept_ref, left_ref, gg_ref, gu_ref, out_ref, grad_ref, other_grad_ref, tiles, grams, sem
):
    core = lax.axis_index("outer")
    pick(core, gg_ref.at[0], gu_ref.at[0], grad_ref, sem.at[0], True)
    pick(core, gu_ref.at[0], gg_ref.at[0], other_grad_ref, sem.at[1], True)
    high = lax.Precision.HIGHEST
    group = groups((R, 128))
    row = lax.broadcasted_iota(jnp.int32, (R, 128), 0)
    lane = lax.broadcasted_iota(jnp.int32, (R, 128), 1)
    half = R // 2
    for f in range(half):
        tiles[8 * f : 8 * f + 8] = line_ref[16 * f : 16 * f + 16].astype(F32)[8:16]
    for odd in range(2):
        gram = tiles[pl.ds(3 * odd, half, stride=8), :]
        for s in range(1, 3):
            gram = gram + tiles[pl.ds(3 * odd + s, half, stride=8), :]
        grams[pl.ds(odd, half, stride=2), :] = gram
    m = jnp.where(group == 0, pltpu.roll(grams[...], 32, 1), 0.0)
    m = jnp.where((group == 1) & (row == lane % R), 1.0, m)
    pivots = jnp.ones((R, 128), F32)
    for first in range(0, R, BLOCK):
        columns = [jnp.broadcast_to(m[:, k : k + 1], (R, 128)) for k in range(first, first + BLOCK)]
        rows = [m[k : k + 1] for k in range(first, first + BLOCK)]
        for i in range(BLOCK):
            k = first + i
            pivot = columns[i][k : k + 1]
            pivots = jnp.where(row == k, pivot, pivots)
            factor = jnp.where(row > k, columns[i] * (1.0 / pivot), 0.0)
            for j in range(i + 1, BLOCK):
                columns[j] = columns[j] - factor * columns[j][k : k + 1]
                at = first + j
                rows[j] = rows[j] - factor[at : at + 1] * rows[i]
            m = m - factor * rows[i]
    scale = lax.rsqrt(pivots)
    scale = scale * (1.5 - 0.5 * pivots * scale * scale)
    one = jnp.where(group == 1, m * scale, 0.0)
    one = one + pltpu.roll(one, 64, 1)
    one = one + pltpu.roll(one, 32, 1)
    u = kept_ref[...]
    rows = []
    for t in range(7):
        h, q = divmod(t, 4)
        rows.append(jnp.where(groups((TILE, 128)) == q, u[8 * h : 8 * h + 8], 0.0))
    rows.append(jnp.zeros((128 - W, 128), F32))
    nexts = dot(one, jnp.concatenate(rows, axis=0), 1, 1, high)
    left = jnp.where(group == 0, left_ref[...].astype(F32), 0.0)
    tall = jnp.concatenate([one, one, one, one], axis=0)
    factors = dot(left, tall, 1, 1, high)
    out_ref[0:R] = jnp.where(lane < 64, nexts, factors)
    out_ref[R : 2 * R] = dot(factors[:, 0:R], one, 1, 0, high)
    pick(core, gg_ref.at[0], gu_ref.at[0], grad_ref, sem.at[0], False)
    pick(core, gu_ref.at[0], gg_ref.at[0], other_grad_ref, sem.at[1], False)


CUTS = (4, 7, 8)


def residual(sizes, sums_ref, side, grad, resid, gate, up, at, sem):
    top = side.astype(BF)
    rest = (side - top.astype(F32)).astype(BF)
    side = jnp.concatenate([top, rest], axis=0)
    none = jnp.zeros_like(side)
    side = jnp.concatenate(
        [jnp.concatenate([side, none], axis=1), jnp.concatenate([none, side], axis=1)], axis=0
    )
    pair_group = groups((16, 128))
    second = lax.broadcasted_iota(jnp.int32, (16, 128), 0) >= 8
    masks = []
    for v in range(7):
        a, b = (2 * v) % 7, (2 * v + 1) % 7
        masks.append(jnp.where(pair_group == jnp.where(second, b % 4, a % 4), 1.0, 0.0).astype(BF))
    wide = 2 * PERIOD
    steps = sums_ref.shape[0] // 512
    edges = [0, *(e * steps // 8 for e in CUTS)]
    parts = [pl.ds(a * wide, (b - a) * wide) for a, b in zip(edges, edges[1:]) if b > a]
    spans = [range(a, b) for a, b in zip(edges, edges[1:]) if b > a]
    for cut, part in enumerate(parts):
        for k in spans[cut]:
            halves = []
            for half in range(2):
                tiles = []
                for d in range(32 * k + 16 * half, 32 * k + 16 * half + 16):
                    at_d = 16 * place(d, sizes)
                    x = sums_ref[at_d : at_d + 16, :]
                    tiles += [x[0:8]] * 4 + [x[8:16]] * 3
                rows = []
                for v in range(56):
                    pair = jnp.concatenate(tiles[2 * v : 2 * v + 2], axis=0)
                    rows.append(pair * masks[v % 7])
                halves.append(jnp.concatenate(rows, axis=0))
            both = dot(side, jnp.concatenate(halves, axis=1), 1, 1)
            for half in range(2):
                product = both[64 * half : 64 * half + R] + both[64 * half + R : 64 * half + 64]
                columns = pl.ds(k * wide + half * PERIOD, PERIOD)
                resid[:, columns] = (grad[:, columns].astype(F32) - product).astype(BF)

        @pl.when(at == 0)
        def _():
            pltpu.make_async_copy(resid.at[:, part], gate.at[0, :, part], sem.at[cut]).start()

        @pl.when(at != 0)
        def _():
            pltpu.make_async_copy(resid.at[:, part], up.at[0, :, part], sem.at[cut]).start()

    for cut, part in enumerate(parts):
        pltpu.make_async_copy(resid.at[:, part], gate.at[0, :, part], sem.at[cut]).wait()


def own_kernel(
    sizes, sums_ref, own_ref, other_ref, grad,
    ng_ref, nu_ref, fg_ref, fu_ref, rg_ref, ru_ref, resid, sem_out,
):
    core = lax.axis_index("outer")
    own, other = own_ref[0:R], other_ref[0:R]
    gate, up = jnp.where(core == 0, own, other), jnp.where(core == 0, other, own)
    ng_ref[...] = gate[:, 0:W]
    nu_ref[...] = up[:, 0:W]
    fg_ref[...] = gate[:, 64 : 64 + R]
    fu_ref[...] = up[:, 64 : 64 + R]
    residual(sizes, sums_ref, own_ref[R : 2 * R], grad, resid, rg_ref, ru_ref, core, sem_out)


def other_kernel(sizes, sums_ref, other_ref, grad, rg_in, ru_in, rg_ref, ru_ref, resid, sem_out):
    del rg_in, ru_in
    core = lax.axis_index("outer")
    residual(sizes, sums_ref, other_ref[R : 2 * R], grad, resid, rg_ref, ru_ref, 1 - core, sem_out)


def call(kernel, outs, scratch, spaces_in, spaces_out, cost, limit, aliases={}):
    space = {"h": pltpu.HBM, "v": pltpu.VMEM}
    specs_out = tuple(pl.BlockSpec(memory_space=space[s]) for s in spaces_out)
    run = pl.pallas_call(
        kernel,
        out_shape=[
            pltpu.HBM(o.shape, o.dtype) if s == "h" and not INTERPRET else o
            for s, o in zip(spaces_out, outs)
        ],
        in_specs=[pl.BlockSpec(memory_space=space[s]) for s in spaces_in],
        out_specs=specs_out,
        scratch_shapes=scratch,
        input_output_aliases=aliases,
        cost_estimate=pl.CostEstimate(flops=cost, bytes_accessed=cost // 16, transcendentals=0),
        compiler_params=pltpu.CompilerParams(vmem_limit_bytes=limit << 20),
        interpret=INTERPRET,
    )

    def pinned(*args):
        return run(
            *(
                pltpu.with_memory_space_constraint(x, pltpu.HBM) if s == "h" and not INTERPRET else x
                for s, x in zip(spaces_in, args)
            )
        )

    return pinned


def shape(dims, dtype):
    return jax.ShapeDtypeStruct(dims, dtype)


def local(grad_gate, grad_up, basis_gate, basis_up):
    sizes = tuple(lax.axis_size(a) for a in ROW)
    near, far = lax.axis_size(NEAR), lax.axis_size(FAR)
    columns = grad_gate.shape[2]
    packed_rows = 16 * near * far
    swap = [(0, 1), (1, 0)]
    dma = pltpu.SemaphoreType.DMA

    def exchange(x, axes):
        return lax.all_to_all(x, axes, 0, 0, tiled=True)

    def gather_far(block):
        return exchange(block, FAR).reshape(16 * far, 128)

    def gather_near(line):
        copies = jnp.broadcast_to(line[None], (near, 16 * far, 128))
        return exchange(copies, NEAR).reshape(packed_rows, 128)

    block, send = call(
        prepare_kernel,
        (shape((far, 16, 128), BF), shape((R, columns), BF)),
        [pltpu.VMEM((R, W), BF), dma((2,))],
        "hhhh",
        "vv",
        1 << 20,
        6,
    )(basis_gate, basis_up, grad_gate, grad_up)
    other = lax.ppermute(send, "outer", swap)
    packed, turned = call(
        functools.partial(pack_kernel, sizes),
        (shape((packed_rows, 256), BF), shape((256, packed_rows), BF)),
        [pltpu.VMEM((R, columns), BF), pltpu.VMEM((packed_rows, 256), BF), dma((2,))],
        "hhv",
        "hv",
        1 << 26,
        16,
    )(grad_gate, grad_up, other)
    basis = gather_near(gather_far(block))
    sums, left = call(
        functools.partial(products_kernel, far),
        (shape((packed_rows, 128), BF), shape((R, 128), BF)),
        [pltpu.VMEM((packed_rows, 256), BF), dma((packed_rows // 512,))],
        "vvh",
        "vv",
        1 << 26,
        16,
    )(basis, turned, packed)
    parts = exchange(sums.reshape(near, 16 * far, 128), NEAR)
    (halfway,) = call(halfway_kernel, (shape((16 * far, 128), BF),), [], "v", "v", 1 << 20, 8)(parts)
    parts = exchange(halfway.reshape(far, 16, 128), FAR)
    block, kept = call(
        total_kernel,
        (shape((far, 16, 128), BF), shape((16, 128), F32)),
        [],
        "v",
        "vv",
        1 << 20,
        4,
    )(parts)
    line = gather_far(block)
    natural = shape((R, columns), BF)
    own, own_grad, other_grad = call(
        solve_kernel,
        (shape((2 * R, 128), F32), natural, natural),
        [pltpu.VMEM((128, 128), F32), pltpu.VMEM((R, 128), F32), dma((2,))],
        "vvvhh",
        "vvv",
        1 << 26,
        4,
    )(line, kept, left, grad_gate, grad_up)
    other = lax.ppermute(own, "outer", swap)
    sums, other = lax.optimization_barrier((gather_near(line), other))
    sums_other = lax.ppermute(sums, "outer", swap)
    working = pltpu.VMEM((R, columns), BF)
    resids = (shape(grad_gate.shape, BF), shape(grad_gate.shape, BF))
    *small, rg, ru = call(
        functools.partial(own_kernel, sizes),
        (shape((R, W), F32), shape((R, W), F32), shape((R, R), F32), shape((R, R), F32), *resids),
        [working, dma((len(CUTS),))],
        "vvvv",
        "vvvvhh",
        1 << 26,
        12,
    )(sums, own, other, own_grad)
    rg, ru = call(
        functools.partial(other_kernel, sizes),
        resids,
        [working, dma((len(CUTS),))],
        "vvvhh",
        "hh",
        1 << 26,
        12,
        {3: 0, 4: 1},
    )(sums_other, other, other_grad, rg, ru)
    return (*small, rg, ru)


def solution(mesh):
    rows = mesh.shape["row"]
    sizes = (4, 2, 4, 2, 4) if rows == 256 else (4, 1, 4, 1, rows // 16)
    finer = Mesh(mesh.devices.reshape(mesh.shape["outer"], *sizes), ("outer", *ROW))
    return jax.shard_map(
        local,
        mesh=finer,
        in_specs=(P("outer", ROW, None), P("outer", ROW, None), P(None, ROW), P(None, ROW)),
        out_specs=(
            P(None, ROW), P(None, ROW), P(ROW, None), P(ROW, None),
            P("outer", ROW, None), P("outer", ROW, None),
        ),
        check_vma=False,
    )
```

```python
import functools

import jax
import jax.numpy as jnp
from jax import lax
from jax.experimental import pallas as pl
from jax.experimental.pallas import tpu as pltpu
from jax.sharding import Mesh
from jax.sharding import PartitionSpec as P

ROW = ("yq", "yp", "zq", "zp", "xq", "xp")
ALL = ("outer", *ROW)
FAR = ("yq", "zq", "xq")
BF = jnp.bfloat16
F32 = jnp.float32
R = 32
W = 56
BLOCK = 4
TILE = 8
PERIOD = 16 * W
INTERPRET = False


def place(d, sizes):
    at = []
    for size in sizes[::-1]:
        at.append(d % size)
        d = d // size
    xp, xq, zp, zq, yp, yq = at
    near = (yp * sizes[3] + zp) * sizes[5] + xp
    return ((near * sizes[0] + yq) * sizes[2] + zq) * sizes[4] + xq


def near_groups(sizes):
    rows = sizes[0] * sizes[1], sizes[2] * sizes[3], sizes[4] * sizes[5]
    found = []
    for core in range(2):
        lines = []
        for n, (many, few) in zip(rows, (sizes[0:2], sizes[2:4], sizes[4:6])):
            shift = core if few == 2 else 0
            lines.append(
                [
                    sorted(((few * q + i + shift) % n for i in range(few)), key=lambda v: v % few)
                    for q in range(many)
                ]
            )
        for ys in lines[0]:
            for zs in lines[1]:
                for xs in lines[2]:
                    found.append(
                        [
                            ((core * rows[0] + y) * rows[1] + z) * rows[2] + x
                            for y in ys
                            for z in zs
                            for x in xs
                        ]
                    )
    return found


def groups(shape):
    return lax.broadcasted_iota(jnp.int32, shape, 1) // R


def three_terms(x):
    high = x.astype(BF).astype(F32)
    middle = (x - high).astype(BF).astype(F32)
    low = (x - high - middle).astype(BF).astype(F32)
    return high, middle, low


def dot(a, b, ca, cb, precision=None):
    return lax.dot_general(
        a, b, (((ca,), (cb,)), ((), ())), precision=precision, preferred_element_type=F32
    )


def prepare_kernel(bg_ref, bu_ref, gg_ref, gu_ref, block_ref, send_ref, basis, sem):
    core = lax.axis_index("outer")

    @pl.when(core == 0)
    def _():
        pltpu.make_async_copy(bg_ref, basis, sem.at[0]).start()
        pltpu.make_async_copy(gu_ref.at[0], send_ref, sem.at[1]).start()

    @pl.when(core != 0)
    def _():
        pltpu.make_async_copy(bu_ref, basis, sem.at[0]).start()
        pltpu.make_async_copy(gg_ref.at[0], send_ref, sem.at[1]).start()

    pltpu.make_async_copy(bg_ref, basis, sem.at[0]).wait()
    turned = basis[...].astype(F32).T
    empty = jnp.zeros((TILE, R), F32)
    rows = []
    for h in range(2):
        tiles = [turned[8 * t : 8 * t + 8] if t < 7 else empty for t in range(4 * h, 4 * h + 4)]
        rows.append(jnp.concatenate(tiles, axis=1))
    block = jnp.concatenate(rows, axis=0).astype(BF)
    block_ref[...] = jnp.broadcast_to(block[None], block_ref.shape)
    pltpu.make_async_copy(gg_ref.at[0], send_ref, sem.at[1]).wait()


def pack_kernel(sizes, gg_ref, gu_ref, other_ref, packed_ref, turned_ref, own, work, sem):
    core = lax.axis_index("outer")

    @pl.when(core == 0)
    def _():
        pltpu.make_async_copy(gg_ref.at[0], own, sem.at[0]).start()

    @pl.when(core != 0)
    def _():
        pltpu.make_async_copy(gu_ref.at[0], own, sem.at[0]).start()

    pltpu.make_async_copy(gg_ref.at[0], own, sem.at[0]).wait()
    empty = jnp.zeros((TILE, 2 * R), F32)

    @pl.loop(0, packed_ref.shape[0] // 256)
    def _(k):
        columns = pl.ds(pl.multiple_of(k * PERIOD, 128), PERIOD)
        x = jnp.concatenate(
            [own[:, columns].astype(F32), other_ref[:, columns].astype(F32)], axis=0
        )
        xt = x.T
        first = place(16 * k, sizes)
        for d in range(16):
            rows = []
            for h in range(2):
                tiles = []
                for t in range(4 * h, 4 * h + 4):
                    at = 8 * (7 * d + t)
                    tiles.append(xt[at : at + 8] if t < 7 else empty)
                rows.append(jnp.concatenate(tiles, axis=1))
            to = pl.multiple_of(16 * (first + place(d, sizes)), 16)
            work[pl.ds(to, 16), :] = jnp.concatenate(rows, axis=0).astype(BF)

    keep = pltpu.make_async_copy(work, packed_ref, sem.at[1])
    keep.start()

    @pl.loop(0, packed_ref.shape[0] // 256)
    def _(k):
        part = pl.ds(pl.multiple_of(k * 256, 256), 256)
        turned_ref[:, part] = work[part, :].astype(F32).T.astype(BF)

    keep.wait()


def products_kernel(far, basis_ref, turned_ref, packed_ref, sums_ref, left_ref, packed, sem):
    step = 512
    loads = []
    for k in range(packed_ref.shape[0] // step):
        part = pl.ds(k * step, step)
        loads.append(pltpu.make_async_copy(packed_ref.at[part], packed.at[part], sem.at[k]))
        loads[-1].start()
    partial = dot(turned_ref[...], basis_ref[...], 1, 0)
    group = groups((R, 128))
    total = jnp.zeros((R, 128), F32)
    for q in range(4):
        slab = partial[64 * q : 64 * q + R] + partial[64 * q + R : 64 * q + 64]
        total = total + jnp.where(group == q, slab, 0.0)
    total = total + pltpu.roll(total, 64, 1)
    total = total + pltpu.roll(total, 32, 1)
    left = (0.5 * total).astype(BF)
    left_ref[...] = left
    wide = left.astype(F32)
    pieces = []
    for q in range(4):
        one = jnp.where(group == q, wide, 0.0)
        pieces += [one, one]
    spread = jnp.concatenate(pieces, axis=0).astype(BF)
    for load in loads:
        load.wait()
    gram = dot(left, left, 0, 0)[0:R]
    terms = three_terms(jnp.where(group == 3, gram, 0.0))
    row = lax.broadcasted_iota(jnp.int32, (TILE, 128), 0)
    empty = jnp.zeros((TILE, 128), F32)
    extra = []
    each = R // far
    for f in range(far):
        tile = empty
        for s in range(3 * each):
            at = each * f + s // 3
            tile = jnp.where(row == s, terms[s % 3][at : at + 1], tile)
        extra.append(tile)
    tiles = []
    for e in range(step // 16):
        tiles += [empty, extra[e % far]]
    added = jnp.concatenate(tiles, axis=0)
    for k in range(len(loads)):
        out = dot(packed[pl.ds(k * step, step), :], spread, 1, 0)
        sums_ref[pl.ds(k * step, step), :] = (out + added).astype(BF)


def summed(parts_ref, scale):
    count, rows, _ = parts_ref.shape

    def add(k, acc):
        return acc + parts_ref[k].astype(F32)

    acc = lax.fori_loop(0, count, add, jnp.zeros((rows, 128), F32), unroll=4)
    acc = acc.reshape(rows // 16, 16, 128)
    row = lax.broadcasted_iota(jnp.int32, acc.shape, 1)
    lane = lax.broadcasted_iota(jnp.int32, acc.shape, 2)
    term = jnp.zeros_like(acc)
    for first in (8, 11):
        gram = acc[:, first : first + 1] + acc[:, first + 1 : first + 2] + acc[:, first + 2 : first + 3]
        for s, part in enumerate(three_terms(gram)):
            term = jnp.where(row == first + s, part, term)
    out = jnp.where((row >= 8) & (lane >= 96), term, scale * acc)
    return out.reshape(rows, 128)


def halfway_kernel(parts_ref, out_ref):
    out_ref[...] = summed(parts_ref, 1.0).astype(BF)


def total_kernel(parts_ref, block_ref, kept_ref):
    out = summed(parts_ref, 0.5)
    block_ref[...] = jnp.broadcast_to(out.astype(BF)[None], block_ref.shape)
    kept_ref[...] = out


def pick(core, first, second, to, sem, start):
    if not start:
        pltpu.make_async_copy(first, to, sem).wait()
        return

    @pl.when(core == 0)
    def _():
        pltpu.make_async_copy(first, to, sem).start()

    @pl.when(core != 0)
    def _():
        pltpu.make_async_copy(second, to, sem).start()


def solve_kernel(
    far, line_ref, kept_ref, left_ref, gg_ref, gu_ref, out_ref, grad_ref, other_grad_ref, tiles, grams, sem
):
    core = lax.axis_index("outer")
    pick(core, gg_ref.at[0], gu_ref.at[0], grad_ref, sem.at[0], True)
    pick(core, gu_ref.at[0], gg_ref.at[0], other_grad_ref, sem.at[1], True)
    high = lax.Precision.HIGHEST
    group = groups((R, 128))
    row = lax.broadcasted_iota(jnp.int32, (R, 128), 0)
    lane = lax.broadcasted_iota(jnp.int32, (R, 128), 1)
    each = R // far
    for f in range(far):
        tiles[8 * f : 8 * f + 8] = line_ref[16 * f : 16 * f + 16].astype(F32)[8:16]
    for i in range(each):
        gram = tiles[pl.ds(3 * i, far, stride=8), :]
        for s in range(1, 3):
            gram = gram + tiles[pl.ds(3 * i + s, far, stride=8), :]
        grams[pl.ds(i, far, stride=each), :] = gram
    m = jnp.where(group == 0, pltpu.roll(grams[...], 32, 1), 0.0)
    m = jnp.where((group == 1) & (row == lane % R), 1.0, m)
    pivots = jnp.ones((R, 128), F32)
    for first in range(0, R, BLOCK):
        columns = [jnp.broadcast_to(m[:, k : k + 1], (R, 128)) for k in range(first, first + BLOCK)]
        rows = [m[k : k + 1] for k in range(first, first + BLOCK)]
        for i in range(BLOCK):
            k = first + i
            pivot = columns[i][k : k + 1]
            pivots = jnp.where(row == k, pivot, pivots)
            factor = jnp.where(row > k, columns[i] * (1.0 / pivot), 0.0)
            for j in range(i + 1, BLOCK):
                columns[j] = columns[j] - factor * columns[j][k : k + 1]
                at = first + j
                rows[j] = rows[j] - factor[at : at + 1] * rows[i]
            m = m - factor * rows[i]
    scale = lax.rsqrt(pivots)
    scale = scale * (1.5 - 0.5 * pivots * scale * scale)
    one = jnp.where(group == 1, m * scale, 0.0)
    one = one + pltpu.roll(one, 64, 1)
    one = one + pltpu.roll(one, 32, 1)
    u = kept_ref[...]
    rows = []
    for t in range(7):
        h, q = divmod(t, 4)
        rows.append(jnp.where(groups((TILE, 128)) == q, u[8 * h : 8 * h + 8], 0.0))
    rows.append(jnp.zeros((128 - W, 128), F32))
    nexts = dot(one, jnp.concatenate(rows, axis=0), 1, 1, high)
    left = jnp.where(group == 0, left_ref[...].astype(F32), 0.0)
    tall = jnp.concatenate([one, one, one, one], axis=0)
    factors = dot(left, tall, 1, 1, high)
    out_ref[0:R] = jnp.where(lane < 64, nexts, factors)
    out_ref[R : 2 * R] = dot(factors[:, 0:R], one, 1, 0, high)
    pick(core, gg_ref.at[0], gu_ref.at[0], grad_ref, sem.at[0], False)
    pick(core, gu_ref.at[0], gg_ref.at[0], other_grad_ref, sem.at[1], False)


SIZES = (4, 2, 4, 2, 2, 2)
CUTS = (4, 7, 8)


def residual(sizes, sums_ref, side, grad, resid, gate, up, at, sem):
    top = side.astype(BF)
    rest = (side - top.astype(F32)).astype(BF)
    side = jnp.concatenate([top, rest], axis=0)
    none = jnp.zeros_like(side)
    side = jnp.concatenate(
        [jnp.concatenate([side, none], axis=1), jnp.concatenate([none, side], axis=1)], axis=0
    )
    pair_group = groups((16, 128))
    second = lax.broadcasted_iota(jnp.int32, (16, 128), 0) >= 8
    masks = []
    for v in range(7):
        a, b = (2 * v) % 7, (2 * v + 1) % 7
        masks.append(jnp.where(pair_group == jnp.where(second, b % 4, a % 4), 1.0, 0.0).astype(BF))
    wide = 2 * PERIOD
    steps = sums_ref.shape[0] // 512
    edges = [0, *(e * steps // 8 for e in CUTS)]
    parts = [pl.ds(a * wide, (b - a) * wide) for a, b in zip(edges, edges[1:]) if b > a]
    spans = [range(a, b) for a, b in zip(edges, edges[1:]) if b > a]
    for cut, part in enumerate(parts):
        for k in spans[cut]:
            halves = []
            for half in range(2):
                tiles = []
                for d in range(32 * k + 16 * half, 32 * k + 16 * half + 16):
                    at_d = 16 * place(d, sizes)
                    x = sums_ref[at_d : at_d + 16, :]
                    tiles += [x[0:8]] * 4 + [x[8:16]] * 3
                rows = []
                for v in range(56):
                    pair = jnp.concatenate(tiles[2 * v : 2 * v + 2], axis=0)
                    rows.append(pair * masks[v % 7])
                halves.append(jnp.concatenate(rows, axis=0))
            both = dot(side, jnp.concatenate(halves, axis=1), 1, 1)
            for half in range(2):
                product = both[64 * half : 64 * half + R] + both[64 * half + R : 64 * half + 64]
                columns = pl.ds(k * wide + half * PERIOD, PERIOD)
                resid[:, columns] = (grad[:, columns].astype(F32) - product).astype(BF)

        @pl.when(at == 0)
        def _():
            pltpu.make_async_copy(resid.at[:, part], gate.at[0, :, part], sem.at[cut]).start()

        @pl.when(at != 0)
        def _():
            pltpu.make_async_copy(resid.at[:, part], up.at[0, :, part], sem.at[cut]).start()

    for cut, part in enumerate(parts):
        pltpu.make_async_copy(resid.at[:, part], gate.at[0, :, part], sem.at[cut]).wait()


def own_kernel(
    sizes, sums_ref, own_ref, other_ref, grad,
    ng_ref, nu_ref, fg_ref, fu_ref, rg_ref, ru_ref, resid, sem_out,
):
    core = lax.axis_index("outer")
    own, other = own_ref[0:R], other_ref[0:R]
    gate, up = jnp.where(core == 0, own, other), jnp.where(core == 0, other, own)
    ng_ref[...] = gate[:, 0:W]
    nu_ref[...] = up[:, 0:W]
    fg_ref[...] = gate[:, 64 : 64 + R]
    fu_ref[...] = up[:, 64 : 64 + R]
    residual(sizes, sums_ref, own_ref[R : 2 * R], grad, resid, rg_ref, ru_ref, core, sem_out)


def other_kernel(sizes, sums_ref, other_ref, grad, rg_in, ru_in, rg_ref, ru_ref, resid, sem_out):
    del rg_in, ru_in
    core = lax.axis_index("outer")
    residual(sizes, sums_ref, other_ref[R : 2 * R], grad, resid, rg_ref, ru_ref, 1 - core, sem_out)


def call(kernel, outs, scratch, spaces_in, spaces_out, cost, limit, aliases={}):
    space = {"h": pltpu.HBM, "v": pltpu.VMEM}
    specs_out = tuple(pl.BlockSpec(memory_space=space[s]) for s in spaces_out)
    run = pl.pallas_call(
        kernel,
        out_shape=[
            pltpu.HBM(o.shape, o.dtype) if s == "h" and not INTERPRET else o
            for s, o in zip(spaces_out, outs)
        ],
        in_specs=[pl.BlockSpec(memory_space=space[s]) for s in spaces_in],
        out_specs=specs_out,
        scratch_shapes=scratch,
        input_output_aliases=aliases,
        cost_estimate=pl.CostEstimate(flops=cost, bytes_accessed=cost // 16, transcendentals=0),
        compiler_params=pltpu.CompilerParams(vmem_limit_bytes=limit << 20),
        interpret=INTERPRET,
    )

    def pinned(*args):
        return run(
            *(
                pltpu.with_memory_space_constraint(x, pltpu.HBM) if s == "h" and not INTERPRET else x
                for s, x in zip(spaces_in, args)
            )
        )

    return pinned


def shape(dims, dtype):
    return jax.ShapeDtypeStruct(dims, dtype)


def local(grad_gate, grad_up, basis_gate, basis_up):
    sizes = tuple(lax.axis_size(a) for a in ROW)
    far = lax.axis_size(FAR)
    near = sizes[1] * sizes[3] * sizes[5]
    pairs = near_groups(sizes)
    columns = grad_gate.shape[2]
    packed_rows = 16 * near * far
    swap = [(0, 1), (1, 0)]
    dma = pltpu.SemaphoreType.DMA

    def exchange_far(x):
        return lax.all_to_all(x, FAR, 0, 0, tiled=True)

    def exchange_near(x):
        return lax.all_to_all(x, ALL, 0, 0, tiled=True, axis_index_groups=pairs)

    def gather_far(block):
        return exchange_far(block).reshape(16 * far, 128)

    def gather_near(line):
        copies = jnp.broadcast_to(line[None], (near, 16 * far, 128))
        return exchange_near(copies).reshape(packed_rows, 128)

    block, send = call(
        prepare_kernel,
        (shape((far, 16, 128), BF), shape((R, columns), BF)),
        [pltpu.VMEM((R, W), BF), dma((2,))],
        "hhhh",
        "vv",
        1 << 20,
        6,
    )(basis_gate, basis_up, grad_gate, grad_up)
    other = lax.ppermute(send, "outer", swap)
    packed, turned = call(
        functools.partial(pack_kernel, sizes),
        (shape((packed_rows, 256), BF), shape((256, packed_rows), BF)),
        [pltpu.VMEM((R, columns), BF), pltpu.VMEM((packed_rows, 256), BF), dma((2,))],
        "hhv",
        "hv",
        1 << 26,
        16,
    )(grad_gate, grad_up, other)
    basis = gather_near(gather_far(block))
    sums, left = call(
        functools.partial(products_kernel, far),
        (shape((packed_rows, 128), BF), shape((R, 128), BF)),
        [pltpu.VMEM((packed_rows, 256), BF), dma((packed_rows // 512,))],
        "vvh",
        "vv",
        1 << 26,
        16,
    )(basis, turned, packed)
    parts = exchange_near(sums.reshape(near, 16 * far, 128))
    (halfway,) = call(halfway_kernel, (shape((16 * far, 128), BF),), [], "v", "v", 1 << 20, 8)(parts)
    parts = exchange_far(halfway.reshape(far, 16, 128))
    block, kept = call(
        total_kernel,
        (shape((far, 16, 128), BF), shape((16, 128), F32)),
        [],
        "v",
        "vv",
        1 << 20,
        4,
    )(parts)
    line = gather_far(block)
    natural = shape((R, columns), BF)
    own, own_grad, other_grad = call(
        functools.partial(solve_kernel, far),
        (shape((2 * R, 128), F32), natural, natural),
        [pltpu.VMEM((8 * far, 128), F32), pltpu.VMEM((R, 128), F32), dma((2,))],
        "vvvhh",
        "vvv",
        1 << 26,
        4,
    )(line, kept, left, grad_gate, grad_up)
    other = lax.ppermute(own, "outer", swap)
    sums, other = lax.optimization_barrier((gather_near(line), other))
    sums_other = lax.ppermute(sums, "outer", swap)
    working = pltpu.VMEM((R, columns), BF)
    resids = (shape(grad_gate.shape, BF), shape(grad_gate.shape, BF))
    *small, rg, ru = call(
        functools.partial(own_kernel, sizes),
        (shape((R, W), F32), shape((R, W), F32), shape((R, R), F32), shape((R, R), F32), *resids),
        [working, dma((len(CUTS),))],
        "vvvv",
        "vvvvhh",
        1 << 26,
        12,
    )(sums, own, other, own_grad)
    rg, ru = call(
        functools.partial(other_kernel, sizes),
        resids,
        [working, dma((len(CUTS),))],
        "vvvhh",
        "hh",
        1 << 26,
        12,
        {3: 0, 4: 1},
    )(sums_other, other, other_grad, rg, ru)
    return (*small, rg, ru)


def solution(mesh):
    rows = mesh.shape["row"]
    sizes = SIZES if rows == 256 else (2, 2, 4, 1, 2, rows // 32)
    finer = Mesh(mesh.devices.reshape(mesh.shape["outer"], *sizes), ("outer", *ROW))
    return jax.shard_map(
        local,
        mesh=finer,
        in_specs=(P("outer", ROW, None), P("outer", ROW, None), P(None, ROW), P(None, ROW)),
        out_specs=(
            P(None, ROW), P(None, ROW), P(ROW, None), P(ROW, None),
            P("outer", ROW, None), P("outer", ROW, None),
        ),
        check_vma=False,
    )
```

```python
import functools

import jax
import jax.numpy as jnp
from jax import lax
from jax.experimental import pallas as pl
from jax.experimental.pallas import tpu as pltpu
from jax.sharding import Mesh
from jax.sharding import PartitionSpec as P

ROW = ("yq", "yp", "zq", "zp", "xq", "xp")
ALL = ("outer", *ROW)
FAR = ("yq", "zq", "xq")
BF = jnp.bfloat16
F32 = jnp.float32
R = 32
W = 56
BLOCK = 4
TILE = 8
PERIOD = 16 * W
INTERPRET = False


def place(d, sizes):
    at = []
    for size in sizes[::-1]:
        at.append(d % size)
        d = d // size
    xp, xq, zp, zq, yp, yq = at
    near = (yp * sizes[3] + zp) * sizes[5] + xp
    return ((near * sizes[0] + yq) * sizes[2] + zq) * sizes[4] + xq


def near_groups(sizes):
    rows = sizes[0] * sizes[1], sizes[2] * sizes[3], sizes[4] * sizes[5]
    found = []
    for core in range(2):
        lines = []
        for n, (many, few) in zip(rows, (sizes[0:2], sizes[2:4], sizes[4:6])):
            shift = core if few == 2 else 0
            lines.append(
                [
                    sorted(((few * q + i + shift) % n for i in range(few)), key=lambda v: v % few)
                    for q in range(many)
                ]
            )
        for ys in lines[0]:
            for zs in lines[1]:
                for xs in lines[2]:
                    found.append(
                        [
                            ((core * rows[0] + y) * rows[1] + z) * rows[2] + x
                            for y in ys
                            for z in zs
                            for x in xs
                        ]
                    )
    return found


def groups(shape):
    return lax.broadcasted_iota(jnp.int32, shape, 1) // R


def three_terms(x):
    high = x.astype(BF).astype(F32)
    middle = (x - high).astype(BF).astype(F32)
    low = (x - high - middle).astype(BF).astype(F32)
    return high, middle, low


def dot(a, b, ca, cb, precision=None):
    return lax.dot_general(
        a, b, (((ca,), (cb,)), ((), ())), precision=precision, preferred_element_type=F32
    )


def prepare_kernel(bg_ref, bu_ref, gg_ref, gu_ref, block_ref, send_ref, basis, sem):
    core = lax.axis_index("outer")

    @pl.when(core == 0)
    def _():
        pltpu.make_async_copy(bg_ref, basis, sem.at[0]).start()
        pltpu.make_async_copy(gu_ref.at[0], send_ref, sem.at[1]).start()

    @pl.when(core != 0)
    def _():
        pltpu.make_async_copy(bu_ref, basis, sem.at[0]).start()
        pltpu.make_async_copy(gg_ref.at[0], send_ref, sem.at[1]).start()

    pltpu.make_async_copy(bg_ref, basis, sem.at[0]).wait()
    turned = basis[...].astype(F32).T
    empty = jnp.zeros((TILE, R), F32)
    rows = []
    for h in range(2):
        tiles = [turned[8 * t : 8 * t + 8] if t < 7 else empty for t in range(4 * h, 4 * h + 4)]
        rows.append(jnp.concatenate(tiles, axis=1))
    block = jnp.concatenate(rows, axis=0).astype(BF)
    block_ref[...] = jnp.broadcast_to(block[None], block_ref.shape)
    pltpu.make_async_copy(gg_ref.at[0], send_ref, sem.at[1]).wait()


def pack_kernel(sizes, gg_ref, gu_ref, other_ref, packed_ref, turned_ref, own, work, sem):
    core = lax.axis_index("outer")

    @pl.when(core == 0)
    def _():
        pltpu.make_async_copy(gg_ref.at[0], own, sem.at[0]).start()

    @pl.when(core != 0)
    def _():
        pltpu.make_async_copy(gu_ref.at[0], own, sem.at[0]).start()

    pltpu.make_async_copy(gg_ref.at[0], own, sem.at[0]).wait()
    empty = jnp.zeros((TILE, 2 * R), F32)

    @pl.loop(0, packed_ref.shape[0] // 256)
    def _(k):
        columns = pl.ds(pl.multiple_of(k * PERIOD, 128), PERIOD)
        x = jnp.concatenate(
            [own[:, columns].astype(F32), other_ref[:, columns].astype(F32)], axis=0
        )
        xt = x.T
        first = place(16 * k, sizes)
        for d in range(16):
            rows = []
            for h in range(2):
                tiles = []
                for t in range(4 * h, 4 * h + 4):
                    at = 8 * (7 * d + t)
                    tiles.append(xt[at : at + 8] if t < 7 else empty)
                rows.append(jnp.concatenate(tiles, axis=1))
            to = pl.multiple_of(16 * (first + place(d, sizes)), 16)
            work[pl.ds(to, 16), :] = jnp.concatenate(rows, axis=0).astype(BF)

    keep = pltpu.make_async_copy(work, packed_ref, sem.at[1])
    keep.start()

    @pl.loop(0, packed_ref.shape[0] // 256)
    def _(k):
        part = pl.ds(pl.multiple_of(k * 256, 256), 256)
        turned_ref[:, part] = work[part, :].astype(F32).T.astype(BF)

    keep.wait()


def products_kernel(far, basis_ref, turned_ref, packed_ref, sums_ref, left_ref, packed, sem):
    step = 512
    loads = []
    for k in range(packed_ref.shape[0] // step):
        part = pl.ds(k * step, step)
        loads.append(pltpu.make_async_copy(packed_ref.at[part], packed.at[part], sem.at[k]))
        loads[-1].start()
    partial = dot(turned_ref[...], basis_ref[...], 1, 0)
    group = groups((R, 128))
    total = jnp.zeros((R, 128), F32)
    for q in range(4):
        slab = partial[64 * q : 64 * q + R] + partial[64 * q + R : 64 * q + 64]
        total = total + jnp.where(group == q, slab, 0.0)
    total = total + pltpu.roll(total, 64, 1)
    total = total + pltpu.roll(total, 32, 1)
    left = (0.5 * total).astype(BF)
    left_ref[...] = left
    wide = left.astype(F32)
    pieces = []
    for q in range(4):
        one = jnp.where(group == q, wide, 0.0)
        pieces += [one, one]
    spread = jnp.concatenate(pieces, axis=0).astype(BF)
    for load in loads:
        load.wait()
    gram = dot(left, left, 0, 0)[0:R]
    terms = three_terms(jnp.where(group == 3, gram, 0.0))
    row = lax.broadcasted_iota(jnp.int32, (TILE, 128), 0)
    empty = jnp.zeros((TILE, 128), F32)
    extra = []
    each = R // far
    for f in range(far):
        tile = empty
        for s in range(3 * each):
            at = each * f + s // 3
            tile = jnp.where(row == s, terms[s % 3][at : at + 1], tile)
        extra.append(tile)
    tiles = []
    for e in range(step // 16):
        tiles += [empty, extra[e % far]]
    added = jnp.concatenate(tiles, axis=0)
    for k in range(len(loads)):
        out = dot(packed[pl.ds(k * step, step), :], spread, 1, 0)
        sums_ref[pl.ds(k * step, step), :] = (out + added).astype(BF)


def summed(parts_ref, scale):
    count, rows, _ = parts_ref.shape

    def add(k, acc):
        return acc + parts_ref[k].astype(F32)

    acc = lax.fori_loop(0, count, add, jnp.zeros((rows, 128), F32), unroll=4)
    acc = acc.reshape(rows // 16, 16, 128)
    row = lax.broadcasted_iota(jnp.int32, acc.shape, 1)
    lane = lax.broadcasted_iota(jnp.int32, acc.shape, 2)
    term = jnp.zeros_like(acc)
    for first in (8, 11):
        gram = acc[:, first : first + 1] + acc[:, first + 1 : first + 2] + acc[:, first + 2 : first + 3]
        for s, part in enumerate(three_terms(gram)):
            term = jnp.where(row == first + s, part, term)
    out = jnp.where((row >= 8) & (lane >= 96), term, scale * acc)
    return out.reshape(rows, 128)


def halfway_kernel(parts_ref, out_ref):
    out_ref[...] = summed(parts_ref, 1.0).astype(BF)


def total_kernel(parts_ref, block_ref, kept_ref):
    out = summed(parts_ref, 0.5)
    block_ref[...] = jnp.broadcast_to(out.astype(BF)[None], block_ref.shape)
    kept_ref[...] = out


def copies_kernel(line_ref, out_ref, sem):
    copies = [pltpu.make_async_copy(line_ref, out_ref.at[k], sem.at[k]) for k in range(out_ref.shape[0])]
    for copy in copies:
        copy.start()
    for copy in copies:
        copy.wait()


def pick(core, first, second, to, sem, start):
    if not start:
        pltpu.make_async_copy(first, to, sem).wait()
        return

    @pl.when(core == 0)
    def _():
        pltpu.make_async_copy(first, to, sem).start()

    @pl.when(core != 0)
    def _():
        pltpu.make_async_copy(second, to, sem).start()


def solve_kernel(
    far, line_ref, kept_ref, left_ref, gg_ref, gu_ref, out_ref, grad_ref, other_grad_ref, tiles, grams, sem
):
    core = lax.axis_index("outer")
    pick(core, gg_ref.at[0], gu_ref.at[0], grad_ref, sem.at[0], True)
    pick(core, gu_ref.at[0], gg_ref.at[0], other_grad_ref, sem.at[1], True)
    high = lax.Precision.HIGHEST
    group = groups((R, 128))
    row = lax.broadcasted_iota(jnp.int32, (R, 128), 0)
    lane = lax.broadcasted_iota(jnp.int32, (R, 128), 1)
    each = R // far
    for f in range(far):
        tiles[8 * f : 8 * f + 8] = line_ref[16 * f : 16 * f + 16].astype(F32)[8:16]
    for i in range(each):
        gram = tiles[pl.ds(3 * i, far, stride=8), :]
        for s in range(1, 3):
            gram = gram + tiles[pl.ds(3 * i + s, far, stride=8), :]
        grams[pl.ds(i, far, stride=each), :] = gram
    m = jnp.where(group == 0, pltpu.roll(grams[...], 32, 1), 0.0)
    m = jnp.where((group == 1) & (row == lane % R), 1.0, m)
    pivots = jnp.ones((R, 128), F32)
    for first in range(0, R, BLOCK):
        columns = [jnp.broadcast_to(m[:, k : k + 1], (R, 128)) for k in range(first, first + BLOCK)]
        rows = [m[k : k + 1] for k in range(first, first + BLOCK)]
        for i in range(BLOCK):
            k = first + i
            pivot = columns[i][k : k + 1]
            pivots = jnp.where(row == k, pivot, pivots)
            factor = jnp.where(row > k, columns[i] * (1.0 / pivot), 0.0)
            for j in range(i + 1, BLOCK):
                columns[j] = columns[j] - factor * columns[j][k : k + 1]
                at = first + j
                rows[j] = rows[j] - factor[at : at + 1] * rows[i]
            m = m - factor * rows[i]
    scale = lax.rsqrt(pivots)
    scale = scale * (1.5 - 0.5 * pivots * scale * scale)
    one = jnp.where(group == 1, m * scale, 0.0)
    one = one + pltpu.roll(one, 64, 1)
    one = one + pltpu.roll(one, 32, 1)
    u = kept_ref[...]
    rows = []
    for t in range(7):
        h, q = divmod(t, 4)
        rows.append(jnp.where(groups((TILE, 128)) == q, u[8 * h : 8 * h + 8], 0.0))
    rows.append(jnp.zeros((128 - W, 128), F32))
    nexts = dot(one, jnp.concatenate(rows, axis=0), 1, 1, high)
    left = jnp.where(group == 0, left_ref[...].astype(F32), 0.0)
    tall = jnp.concatenate([one, one, one, one], axis=0)
    factors = dot(left, tall, 1, 1, high)
    out_ref[0:R] = jnp.where(lane < 64, nexts, factors)
    out_ref[R : 2 * R] = dot(factors[:, 0:R], one, 1, 0, high)
    pick(core, gg_ref.at[0], gu_ref.at[0], grad_ref, sem.at[0], False)
    pick(core, gu_ref.at[0], gg_ref.at[0], other_grad_ref, sem.at[1], False)


SIZES = (4, 2, 4, 2, 1, 4)
CUTS = (4, 7, 8)


def residual(sizes, sums_ref, side, grad, resid, gate, up, at, sem):
    top = side.astype(BF)
    rest = (side - top.astype(F32)).astype(BF)
    side = jnp.concatenate([top, rest], axis=0)
    none = jnp.zeros_like(side)
    side = jnp.concatenate(
        [jnp.concatenate([side, none], axis=1), jnp.concatenate([none, side], axis=1)], axis=0
    )
    pair_group = groups((16, 128))
    second = lax.broadcasted_iota(jnp.int32, (16, 128), 0) >= 8
    masks = []
    for v in range(7):
        a, b = (2 * v) % 7, (2 * v + 1) % 7
        masks.append(jnp.where(pair_group == jnp.where(second, b % 4, a % 4), 1.0, 0.0).astype(BF))
    wide = 2 * PERIOD
    steps = sums_ref.shape[0] // 512
    edges = [0, *(e * steps // 8 for e in CUTS)]
    parts = [pl.ds(a * wide, (b - a) * wide) for a, b in zip(edges, edges[1:]) if b > a]
    spans = [range(a, b) for a, b in zip(edges, edges[1:]) if b > a]
    for cut, part in enumerate(parts):
        for k in spans[cut]:
            halves = []
            for half in range(2):
                tiles = []
                for d in range(32 * k + 16 * half, 32 * k + 16 * half + 16):
                    at_d = 16 * place(d, sizes)
                    x = sums_ref[at_d : at_d + 16, :]
                    tiles += [x[0:8]] * 4 + [x[8:16]] * 3
                rows = []
                for v in range(56):
                    pair = jnp.concatenate(tiles[2 * v : 2 * v + 2], axis=0)
                    rows.append(pair * masks[v % 7])
                halves.append(jnp.concatenate(rows, axis=0))
            both = dot(side, jnp.concatenate(halves, axis=1), 1, 1)
            for half in range(2):
                product = both[64 * half : 64 * half + R] + both[64 * half + R : 64 * half + 64]
                columns = pl.ds(k * wide + half * PERIOD, PERIOD)
                resid[:, columns] = (grad[:, columns].astype(F32) - product).astype(BF)

        @pl.when(at == 0)
        def _():
            pltpu.make_async_copy(resid.at[:, part], gate.at[0, :, part], sem.at[cut]).start()

        @pl.when(at != 0)
        def _():
            pltpu.make_async_copy(resid.at[:, part], up.at[0, :, part], sem.at[cut]).start()

    for cut, part in enumerate(parts):
        pltpu.make_async_copy(resid.at[:, part], gate.at[0, :, part], sem.at[cut]).wait()


def own_kernel(
    sizes, sums_ref, own_ref, other_ref, grad,
    ng_ref, nu_ref, fg_ref, fu_ref, rg_ref, ru_ref, resid, sem_out,
):
    core = lax.axis_index("outer")
    own, other = own_ref[0:R], other_ref[0:R]
    gate, up = jnp.where(core == 0, own, other), jnp.where(core == 0, other, own)
    ng_ref[...] = gate[:, 0:W]
    nu_ref[...] = up[:, 0:W]
    fg_ref[...] = gate[:, 64 : 64 + R]
    fu_ref[...] = up[:, 64 : 64 + R]
    residual(sizes, sums_ref, own_ref[R : 2 * R], grad, resid, rg_ref, ru_ref, core, sem_out)


def other_kernel(sizes, sums_ref, other_ref, grad, rg_in, ru_in, rg_ref, ru_ref, resid, sem_out):
    del rg_in, ru_in
    core = lax.axis_index("outer")
    residual(sizes, sums_ref, other_ref[R : 2 * R], grad, resid, rg_ref, ru_ref, 1 - core, sem_out)


def call(kernel, outs, scratch, spaces_in, spaces_out, cost, limit, aliases={}):
    space = {"h": pltpu.HBM, "v": pltpu.VMEM}
    specs_out = tuple(pl.BlockSpec(memory_space=space[s]) for s in spaces_out)
    run = pl.pallas_call(
        kernel,
        out_shape=[
            pltpu.HBM(o.shape, o.dtype) if s == "h" and not INTERPRET else o
            for s, o in zip(spaces_out, outs)
        ],
        in_specs=[pl.BlockSpec(memory_space=space[s]) for s in spaces_in],
        out_specs=specs_out,
        scratch_shapes=scratch,
        input_output_aliases=aliases,
        cost_estimate=pl.CostEstimate(flops=cost, bytes_accessed=cost // 16, transcendentals=0),
        compiler_params=pltpu.CompilerParams(vmem_limit_bytes=limit << 20),
        interpret=INTERPRET,
    )

    def pinned(*args):
        return run(
            *(
                pltpu.with_memory_space_constraint(x, pltpu.HBM) if s == "h" and not INTERPRET else x
                for s, x in zip(spaces_in, args)
            )
        )

    return pinned


def shape(dims, dtype):
    return jax.ShapeDtypeStruct(dims, dtype)


def local(grad_gate, grad_up, basis_gate, basis_up):
    sizes = tuple(lax.axis_size(a) for a in ROW)
    far = lax.axis_size(FAR)
    near = sizes[1] * sizes[3] * sizes[5]
    pairs = near_groups(sizes)
    columns = grad_gate.shape[2]
    packed_rows = 16 * near * far
    swap = [(0, 1), (1, 0)]
    dma = pltpu.SemaphoreType.DMA

    def exchange_far(x):
        return lax.all_to_all(x, FAR, 0, 0, tiled=True)

    def exchange_near(x):
        return lax.all_to_all(x, ALL, 0, 0, tiled=True, axis_index_groups=pairs)

    def gather_far(block):
        return exchange_far(block).reshape(16 * far, 128)

    def gather_near(line):
        outs = (shape((near, 16 * far, 128), BF),)
        (copies,) = call(copies_kernel, outs, [dma((near,))], "v", "h", 1 << 20, 2)(line)
        return exchange_near(copies).reshape(packed_rows, 128)

    block, send = call(
        prepare_kernel,
        (shape((far, 16, 128), BF), shape((R, columns), BF)),
        [pltpu.VMEM((R, W), BF), dma((2,))],
        "hhhh",
        "vv",
        1 << 20,
        6,
    )(basis_gate, basis_up, grad_gate, grad_up)
    other = lax.ppermute(send, "outer", swap)
    packed, turned = call(
        functools.partial(pack_kernel, sizes),
        (shape((packed_rows, 256), BF), shape((256, packed_rows), BF)),
        [pltpu.VMEM((R, columns), BF), pltpu.VMEM((packed_rows, 256), BF), dma((2,))],
        "hhv",
        "hv",
        1 << 26,
        16,
    )(grad_gate, grad_up, other)
    basis = gather_near(gather_far(block))
    sums, left = call(
        functools.partial(products_kernel, far),
        (shape((packed_rows, 128), BF), shape((R, 128), BF)),
        [pltpu.VMEM((packed_rows, 256), BF), dma((packed_rows // 512,))],
        "vvh",
        "vv",
        1 << 26,
        16,
    )(basis, turned, packed)
    parts = exchange_near(sums.reshape(near, 16 * far, 128))
    (halfway,) = call(halfway_kernel, (shape((16 * far, 128), BF),), [], "v", "v", 1 << 20, 8)(parts)
    parts = exchange_far(halfway.reshape(far, 16, 128))
    block, kept = call(
        total_kernel,
        (shape((far, 16, 128), BF), shape((16, 128), F32)),
        [],
        "v",
        "vv",
        1 << 20,
        4,
    )(parts)
    line = gather_far(block)
    natural = shape((R, columns), BF)
    own, own_grad, other_grad = call(
        functools.partial(solve_kernel, far),
        (shape((2 * R, 128), F32), natural, natural),
        [pltpu.VMEM((8 * far, 128), F32), pltpu.VMEM((R, 128), F32), dma((2,))],
        "vvvhh",
        "vvv",
        1 << 26,
        4,
    )(line, kept, left, grad_gate, grad_up)
    other = lax.ppermute(own, "outer", swap)
    sums, other = lax.optimization_barrier((gather_near(line), other))
    sums_other = lax.ppermute(sums, "outer", swap)
    working = pltpu.VMEM((R, columns), BF)
    resids = (shape(grad_gate.shape, BF), shape(grad_gate.shape, BF))
    *small, rg, ru = call(
        functools.partial(own_kernel, sizes),
        (shape((R, W), F32), shape((R, W), F32), shape((R, R), F32), shape((R, R), F32), *resids),
        [working, dma((len(CUTS),))],
        "vvvv",
        "vvvvhh",
        1 << 26,
        12,
    )(sums, own, other, own_grad)
    rg, ru = call(
        functools.partial(other_kernel, sizes),
        resids,
        [working, dma((len(CUTS),))],
        "vvvhh",
        "hh",
        1 << 26,
        12,
        {3: 0, 4: 1},
    )(sums_other, other, other_grad, rg, ru)
    return (*small, rg, ru)


def solution(mesh):
    rows = mesh.shape["row"]
    sizes = SIZES if rows == 256 else (2, 2, 4, 1, 2, rows // 32)
    finer = Mesh(mesh.devices.reshape(mesh.shape["outer"], *sizes), ("outer", *ROW))
    return jax.shard_map(
        local,
        mesh=finer,
        in_specs=(P("outer", ROW, None), P("outer", ROW, None), P(None, ROW), P(None, ROW)),
        out_specs=(
            P(None, ROW), P(None, ROW), P(ROW, None), P(ROW, None),
            P("outer", ROW, None), P("outer", ROW, None),
        ),
        check_vma=False,
    )
```

```python
import functools

import jax
import jax.numpy as jnp
from jax import lax
from jax.experimental import pallas as pl
from jax.experimental.pallas import tpu as pltpu
from jax.sharding import Mesh
from jax.sharding import PartitionSpec as P

ROW = ("yq", "yp", "zq", "zp", "x")
NEAR = ("x", "yp", "zp")
FAR = ("zq", "yq")
BF = jnp.bfloat16
F32 = jnp.float32
R = 32
W = 56
BLOCK = 4
TILE = 8
PERIOD = 16 * W
INTERPRET = False


def place(d, sizes):
    _, yp, zq, zp, x = sizes
    at_x, d = d % x, d // x
    at_zp, d = d % zp, d // zp
    at_zq, d = d % zq, d // zq
    at_yp, at_yq = d % yp, d // yp
    near = (at_x * yp + at_yp) * zp + at_zp
    return (near * zq + at_zq) * sizes[0] + at_yq


def groups(shape):
    return lax.broadcasted_iota(jnp.int32, shape, 1) // R


def three_terms(x):
    high = x.astype(BF).astype(F32)
    middle = (x - high).astype(BF).astype(F32)
    low = (x - high - middle).astype(BF).astype(F32)
    return high, middle, low


def dot(a, b, ca, cb, precision=None):
    return lax.dot_general(
        a, b, (((ca,), (cb,)), ((), ())), precision=precision, preferred_element_type=F32
    )


def prepare_kernel(bg_ref, bu_ref, gg_ref, gu_ref, block_ref, send_ref, basis, sem):
    core = lax.axis_index("outer")

    @pl.when(core == 0)
    def _():
        pltpu.make_async_copy(bg_ref, basis, sem.at[0]).start()
        pltpu.make_async_copy(gu_ref.at[0], send_ref, sem.at[1]).start()

    @pl.when(core != 0)
    def _():
        pltpu.make_async_copy(bu_ref, basis, sem.at[0]).start()
        pltpu.make_async_copy(gg_ref.at[0], send_ref, sem.at[1]).start()

    pltpu.make_async_copy(bg_ref, basis, sem.at[0]).wait()
    turned = basis[...].astype(F32).T
    empty = jnp.zeros((TILE, R), F32)
    rows = []
    for h in range(2):
        tiles = [turned[8 * t : 8 * t + 8] if t < 7 else empty for t in range(4 * h, 4 * h + 4)]
        rows.append(jnp.concatenate(tiles, axis=1))
    block = jnp.concatenate(rows, axis=0).astype(BF)
    block_ref[...] = jnp.broadcast_to(block[None], block_ref.shape)
    pltpu.make_async_copy(gg_ref.at[0], send_ref, sem.at[1]).wait()


def pack_kernel(sizes, gg_ref, gu_ref, other_ref, packed_ref, turned_ref, own, work, sem):
    core = lax.axis_index("outer")

    @pl.when(core == 0)
    def _():
        pltpu.make_async_copy(gg_ref.at[0], own, sem.at[0]).start()

    @pl.when(core != 0)
    def _():
        pltpu.make_async_copy(gu_ref.at[0], own, sem.at[0]).start()

    pltpu.make_async_copy(gg_ref.at[0], own, sem.at[0]).wait()
    empty = jnp.zeros((TILE, 2 * R), F32)

    @pl.loop(0, packed_ref.shape[0] // 256)
    def _(k):
        columns = pl.ds(pl.multiple_of(k * PERIOD, 128), PERIOD)
        x = jnp.concatenate(
            [own[:, columns].astype(F32), other_ref[:, columns].astype(F32)], axis=0
        )
        xt = x.T
        first = place(16 * k, sizes)
        for d in range(16):
            rows = []
            for h in range(2):
                tiles = []
                for t in range(4 * h, 4 * h + 4):
                    at = 8 * (7 * d + t)
                    tiles.append(xt[at : at + 8] if t < 7 else empty)
                rows.append(jnp.concatenate(tiles, axis=1))
            to = pl.multiple_of(16 * (first + place(d, sizes)), 16)
            work[pl.ds(to, 16), :] = jnp.concatenate(rows, axis=0).astype(BF)

    keep = pltpu.make_async_copy(work, packed_ref, sem.at[1])
    keep.start()

    @pl.loop(0, packed_ref.shape[0] // 256)
    def _(k):
        part = pl.ds(pl.multiple_of(k * 256, 256), 256)
        turned_ref[:, part] = work[part, :].astype(F32).T.astype(BF)

    keep.wait()


def products_kernel(far, basis_ref, turned_ref, packed_ref, sums_ref, left_ref, packed, sem):
    step = 512
    loads = []
    for k in range(packed_ref.shape[0] // step):
        part = pl.ds(k * step, step)
        loads.append(pltpu.make_async_copy(packed_ref.at[part], packed.at[part], sem.at[k]))
        loads[-1].start()
    partial = dot(turned_ref[...], basis_ref[...], 1, 0)
    group = groups((R, 128))
    total = jnp.zeros((R, 128), F32)
    for q in range(4):
        slab = partial[64 * q : 64 * q + R] + partial[64 * q + R : 64 * q + 64]
        total = total + jnp.where(group == q, slab, 0.0)
    total = total + pltpu.roll(total, 64, 1)
    total = total + pltpu.roll(total, 32, 1)
    left = (0.5 * total).astype(BF)
    left_ref[...] = left
    wide = left.astype(F32)
    pieces = []
    for q in range(4):
        one = jnp.where(group == q, wide, 0.0)
        pieces += [one, one]
    spread = jnp.concatenate(pieces, axis=0).astype(BF)
    for load in loads:
        load.wait()
    gram = dot(left, left, 0, 0)[0:R]
    terms = three_terms(jnp.where(group == 3, gram, 0.0))
    row = lax.broadcasted_iota(jnp.int32, (TILE, 128), 0)
    empty = jnp.zeros((TILE, 128), F32)
    extra = []
    for a in range(R // 2):
        tile = empty
        for s in range(6):
            at = 2 * a + s // 3
            tile = jnp.where(row == s, terms[s % 3][at : at + 1], tile)
        extra.append(tile)
    tiles = []
    for e in range(step // 16):
        tiles += [empty, extra[e % far]]
    added = jnp.concatenate(tiles, axis=0)
    for k in range(len(loads)):
        out = dot(packed[pl.ds(k * step, step), :], spread, 1, 0)
        sums_ref[pl.ds(k * step, step), :] = (out + added).astype(BF)


def summed(parts_ref, scale):
    count, rows, _ = parts_ref.shape

    def add(k, acc):
        return acc + parts_ref[k].astype(F32)

    acc = lax.fori_loop(0, count, add, jnp.zeros((rows, 128), F32), unroll=4)
    acc = acc.reshape(rows // 16, 16, 128)
    row = lax.broadcasted_iota(jnp.int32, acc.shape, 1)
    lane = lax.broadcasted_iota(jnp.int32, acc.shape, 2)
    term = jnp.zeros_like(acc)
    for first in (8, 11):
        gram = acc[:, first : first + 1] + acc[:, first + 1 : first + 2] + acc[:, first + 2 : first + 3]
        for s, part in enumerate(three_terms(gram)):
            term = jnp.where(row == first + s, part, term)
    out = jnp.where((row >= 8) & (lane >= 96), term, scale * acc)
    return out.reshape(rows, 128)


def halfway_kernel(parts_ref, out_ref):
    out_ref[...] = summed(parts_ref, 1.0).astype(BF)


def total_kernel(parts_ref, block_ref, kept_ref):
    out = summed(parts_ref, 0.5)
    block_ref[...] = jnp.broadcast_to(out.astype(BF)[None], block_ref.shape)
    kept_ref[...] = out


def pick(core, first, second, to, sem, start):
    if not start:
        pltpu.make_async_copy(first, to, sem).wait()
        return

    @pl.when(core == 0)
    def _():
        pltpu.make_async_copy(first, to, sem).start()

    @pl.when(core != 0)
    def _():
        pltpu.make_async_copy(second, to, sem).start()


def solve_kernel(
    line_ref, kept_ref, left_ref, gg_ref, gu_ref, out_ref, grad_ref, other_grad_ref, tiles, grams, sem
):
    core = lax.axis_index("outer")
    pick(core, gg_ref.at[0], gu_ref.at[0], grad_ref, sem.at[0], True)
    pick(core, gu_ref.at[0], gg_ref.at[0], other_grad_ref, sem.at[1], True)
    high = lax.Precision.HIGHEST
    group = groups((R, 128))
    row = lax.broadcasted_iota(jnp.int32, (R, 128), 0)
    lane = lax.broadcasted_iota(jnp.int32, (R, 128), 1)
    half = R // 2
    for f in range(half):
        tiles[8 * f : 8 * f + 8] = line_ref[16 * f : 16 * f + 16].astype(F32)[8:16]
    for odd in range(2):
        gram = tiles[pl.ds(3 * odd, half, stride=8), :]
        for s in range(1, 3):
            gram = gram + tiles[pl.ds(3 * odd + s, half, stride=8), :]
        grams[pl.ds(odd, half, stride=2), :] = gram
    m = jnp.where(group == 0, pltpu.roll(grams[...], 32, 1), 0.0)
    m = jnp.where((group == 1) & (row == lane % R), 1.0, m)
    pivots = jnp.ones((R, 128), F32)
    for first in range(0, R, BLOCK):
        columns = [jnp.broadcast_to(m[:, k : k + 1], (R, 128)) for k in range(first, first + BLOCK)]
        rows = [m[k : k + 1] for k in range(first, first + BLOCK)]
        for i in range(BLOCK):
            k = first + i
            pivot = columns[i][k : k + 1]
            pivots = jnp.where(row == k, pivot, pivots)
            factor = jnp.where(row > k, columns[i] * (1.0 / pivot), 0.0)
            for j in range(i + 1, BLOCK):
                columns[j] = columns[j] - factor * columns[j][k : k + 1]
                at = first + j
                rows[j] = rows[j] - factor[at : at + 1] * rows[i]
            m = m - factor * rows[i]
    scale = lax.rsqrt(pivots)
    scale = scale * (1.5 - 0.5 * pivots * scale * scale)
    one = jnp.where(group == 1, m * scale, 0.0)
    one = one + pltpu.roll(one, 64, 1)
    one = one + pltpu.roll(one, 32, 1)
    u = kept_ref[...]
    rows = []
    for t in range(7):
        h, q = divmod(t, 4)
        rows.append(jnp.where(groups((TILE, 128)) == q, u[8 * h : 8 * h + 8], 0.0))
    rows.append(jnp.zeros((128 - W, 128), F32))
    nexts = dot(one, jnp.concatenate(rows, axis=0), 1, 1, high)
    left = jnp.where(group == 0, left_ref[...].astype(F32), 0.0)
    tall = jnp.concatenate([one, one, one, one], axis=0)
    factors = dot(left, tall, 1, 1, high)
    out_ref[0:R] = jnp.where(lane < 64, nexts, factors)
    out_ref[R : 2 * R] = dot(factors[:, 0:R], one, 1, 0, high)
    pick(core, gg_ref.at[0], gu_ref.at[0], grad_ref, sem.at[0], False)
    pick(core, gu_ref.at[0], gg_ref.at[0], other_grad_ref, sem.at[1], False)


CUTS = (4, 7, 8)


def residual(sizes, sums_ref, side, grad, resid, gate, up, at, sem):
    top = side.astype(BF)
    rest = (side - top.astype(F32)).astype(BF)
    side = jnp.concatenate([top, rest], axis=0)
    none = jnp.zeros_like(side)
    side = jnp.concatenate(
        [jnp.concatenate([side, none], axis=1), jnp.concatenate([none, side], axis=1)], axis=0
    )
    pair_group = groups((16, 128))
    second = lax.broadcasted_iota(jnp.int32, (16, 128), 0) >= 8
    masks = []
    for v in range(7):
        a, b = (2 * v) % 7, (2 * v + 1) % 7
        masks.append(jnp.where(pair_group == jnp.where(second, b % 4, a % 4), 1.0, 0.0).astype(BF))
    wide = 2 * PERIOD
    steps = sums_ref.shape[0] // 512
    edges = [0, *(e * steps // 8 for e in CUTS)]
    parts = [pl.ds(a * wide, (b - a) * wide) for a, b in zip(edges, edges[1:]) if b > a]
    spans = [range(a, b) for a, b in zip(edges, edges[1:]) if b > a]
    for cut, part in enumerate(parts):
        for k in spans[cut]:
            halves = []
            for half in range(2):
                tiles = []
                for d in range(32 * k + 16 * half, 32 * k + 16 * half + 16):
                    at_d = 16 * place(d, sizes)
                    x = sums_ref[at_d : at_d + 16, :]
                    tiles += [x[0:8]] * 4 + [x[8:16]] * 3
                rows = []
                for v in range(56):
                    pair = jnp.concatenate(tiles[2 * v : 2 * v + 2], axis=0)
                    rows.append(pair * masks[v % 7])
                halves.append(jnp.concatenate(rows, axis=0))
            both = dot(side, jnp.concatenate(halves, axis=1), 1, 1)
            for half in range(2):
                product = both[64 * half : 64 * half + R] + both[64 * half + R : 64 * half + 64]
                columns = pl.ds(k * wide + half * PERIOD, PERIOD)
                resid[:, columns] = (grad[:, columns].astype(F32) - product).astype(BF)

        @pl.when(at == 0)
        def _():
            pltpu.make_async_copy(resid.at[:, part], gate.at[0, :, part], sem.at[cut]).start()

        @pl.when(at != 0)
        def _():
            pltpu.make_async_copy(resid.at[:, part], up.at[0, :, part], sem.at[cut]).start()

    for cut, part in enumerate(parts):
        pltpu.make_async_copy(resid.at[:, part], gate.at[0, :, part], sem.at[cut]).wait()


def own_kernel(
    sizes, sums_ref, own_ref, other_ref, grad,
    ng_ref, nu_ref, fg_ref, fu_ref, rg_ref, ru_ref, resid, sem_out,
):
    core = lax.axis_index("outer")
    own, other = own_ref[0:R], other_ref[0:R]
    gate, up = jnp.where(core == 0, own, other), jnp.where(core == 0, other, own)
    ng_ref[...] = gate[:, 0:W]
    nu_ref[...] = up[:, 0:W]
    fg_ref[...] = gate[:, 64 : 64 + R]
    fu_ref[...] = up[:, 64 : 64 + R]
    residual(sizes, sums_ref, own_ref[R : 2 * R], grad, resid, rg_ref, ru_ref, core, sem_out)


def other_kernel(sizes, sums_ref, other_ref, grad, rg_in, ru_in, rg_ref, ru_ref, resid, sem_out):
    del rg_in, ru_in
    core = lax.axis_index("outer")
    residual(sizes, sums_ref, other_ref[R : 2 * R], grad, resid, rg_ref, ru_ref, 1 - core, sem_out)


def call(kernel, outs, scratch, spaces_in, spaces_out, cost, limit, aliases={}):
    space = {"h": pltpu.HBM, "v": pltpu.VMEM}
    specs_out = tuple(pl.BlockSpec(memory_space=space[s]) for s in spaces_out)
    run = pl.pallas_call(
        kernel,
        out_shape=[
            pltpu.HBM(o.shape, o.dtype) if s == "h" and not INTERPRET else o
            for s, o in zip(spaces_out, outs)
        ],
        in_specs=[pl.BlockSpec(memory_space=space[s]) for s in spaces_in],
        out_specs=specs_out,
        scratch_shapes=scratch,
        input_output_aliases=aliases,
        cost_estimate=pl.CostEstimate(flops=cost, bytes_accessed=cost // 16, transcendentals=0),
        compiler_params=pltpu.CompilerParams(vmem_limit_bytes=limit << 20),
        interpret=INTERPRET,
    )

    def pinned(*args):
        return run(
            *(
                pltpu.with_memory_space_constraint(x, pltpu.HBM) if s == "h" and not INTERPRET else x
                for s, x in zip(spaces_in, args)
            )
        )

    return pinned


def shape(dims, dtype):
    return jax.ShapeDtypeStruct(dims, dtype)


def local(grad_gate, grad_up, basis_gate, basis_up):
    sizes = tuple(lax.axis_size(a) for a in ROW)
    near, far = lax.axis_size(NEAR), lax.axis_size(FAR)
    columns = grad_gate.shape[2]
    packed_rows = 16 * near * far
    swap = [(0, 1), (1, 0)]
    dma = pltpu.SemaphoreType.DMA

    def exchange(x, axes):
        return lax.all_to_all(x, axes, 0, 0, tiled=True)

    def gather_far(block):
        return exchange(block, FAR).reshape(16 * far, 128)

    def gather_near(line):
        copies = jnp.broadcast_to(line[None], (near, 16 * far, 128))
        return exchange(copies, NEAR).reshape(packed_rows, 128)

    block, send = call(
        prepare_kernel,
        (shape((far, 16, 128), BF), shape((R, columns), BF)),
        [pltpu.VMEM((R, W), BF), dma((2,))],
        "hhhh",
        "vv",
        1 << 20,
        6,
    )(basis_gate, basis_up, grad_gate, grad_up)
    other = lax.ppermute(send, "outer", swap)
    packed, turned = call(
        functools.partial(pack_kernel, sizes),
        (shape((packed_rows, 256), BF), shape((256, packed_rows), BF)),
        [pltpu.VMEM((R, columns), BF), pltpu.VMEM((packed_rows, 256), BF), dma((2,))],
        "hhv",
        "hv",
        1 << 26,
        16,
    )(grad_gate, grad_up, other)
    basis = gather_near(gather_far(block))
    sums, left = call(
        functools.partial(products_kernel, far),
        (shape((packed_rows, 128), BF), shape((R, 128), BF)),
        [pltpu.VMEM((packed_rows, 256), BF), dma((packed_rows // 512,))],
        "vvh",
        "vv",
        1 << 26,
        16,
    )(basis, turned, packed)
    parts = exchange(sums.reshape(near, 16 * far, 128), NEAR)
    (halfway,) = call(halfway_kernel, (shape((16 * far, 128), BF),), [], "v", "v", 1 << 20, 8)(parts)
    parts = exchange(halfway.reshape(far, 16, 128), FAR)
    block, kept = call(
        total_kernel,
        (shape((far, 16, 128), BF), shape((16, 128), F32)),
        [],
        "v",
        "vv",
        1 << 20,
        4,
    )(parts)
    line = gather_far(block)
    natural = shape((R, columns), BF)
    own, own_grad, other_grad = call(
        solve_kernel,
        (shape((2 * R, 128), F32), natural, natural),
        [pltpu.VMEM((128, 128), F32), pltpu.VMEM((R, 128), F32), dma((2,))],
        "vvvhh",
        "vvv",
        1 << 26,
        4,
    )(line, kept, left, grad_gate, grad_up)
    other = lax.ppermute(own, "outer", swap)
    sums, other = lax.optimization_barrier((gather_near(line), other))
    sums_other = lax.ppermute(sums, "outer", swap)
    working = pltpu.VMEM((R, columns), BF)
    resids = (shape(grad_gate.shape, BF), shape(grad_gate.shape, BF))
    *small, rg, ru = call(
        functools.partial(own_kernel, sizes),
        (shape((R, W), F32), shape((R, W), F32), shape((R, R), F32), shape((R, R), F32), *resids),
        [working, dma((len(CUTS),))],
        "vvvv",
        "vvvvhh",
        1 << 26,
        12,
    )(sums, own, other, own_grad)
    rg, ru = call(
        functools.partial(other_kernel, sizes),
        resids,
        [working, dma((len(CUTS),))],
        "vvvhh",
        "hh",
        1 << 26,
        12,
        {3: 0, 4: 1},
    )(sums_other, other, other_grad, rg, ru)
    return (*small, rg, ru)


def solution(mesh):
    rows = mesh.shape["row"]
    sizes = (4, 2, 4, 2, 4) if rows == 256 else (4, 1, 4, 1, rows // 16)
    finer = Mesh(mesh.devices.reshape(mesh.shape["outer"], *sizes), ("outer", *ROW))
    return jax.shard_map(
        local,
        mesh=finer,
        in_specs=(P("outer", ROW, None), P("outer", ROW, None), P(None, ROW), P(None, ROW)),
        out_specs=(
            P(None, ROW), P(None, ROW), P(ROW, None), P(ROW, None),
            P("outer", ROW, None), P("outer", ROW, None),
        ),
        check_vma=False,
    )
```

```python
import functools

import jax
import jax.numpy as jnp
from jax import lax
from jax.experimental import pallas as pl
from jax.experimental.pallas import tpu as pltpu
from jax.sharding import Mesh
from jax.sharding import PartitionSpec as P

ROW = ("yq", "yp", "zq", "zp", "x")
NEAR = ("x", "yp", "zp")
FAR = ("zq", "yq")
BF = jnp.bfloat16
F32 = jnp.float32
R = 32
W = 56
BLOCK = 4
TILE = 8
PERIOD = 16 * W
INTERPRET = False


def place(d, sizes):
    _, yp, zq, zp, x = sizes
    at_x, d = d % x, d // x
    at_zp, d = d % zp, d // zp
    at_zq, d = d % zq, d // zq
    at_yp, at_yq = d % yp, d // yp
    near = (at_x * yp + at_yp) * zp + at_zp
    return (near * zq + at_zq) * sizes[0] + at_yq


def groups(shape):
    return lax.broadcasted_iota(jnp.int32, shape, 1) // R


def three_terms(x):
    high = x.astype(BF).astype(F32)
    middle = (x - high).astype(BF).astype(F32)
    low = (x - high - middle).astype(BF).astype(F32)
    return high, middle, low


def dot(a, b, ca, cb, precision=None):
    return lax.dot_general(
        a, b, (((ca,), (cb,)), ((), ())), precision=precision, preferred_element_type=F32
    )


def prepare_kernel(bg_ref, bu_ref, gg_ref, gu_ref, block_ref, send_ref, basis, sem):
    core = lax.axis_index("outer")

    @pl.when(core == 0)
    def _():
        pltpu.make_async_copy(bg_ref, basis, sem.at[0]).start()
        pltpu.make_async_copy(gu_ref.at[0], send_ref, sem.at[1]).start()

    @pl.when(core != 0)
    def _():
        pltpu.make_async_copy(bu_ref, basis, sem.at[0]).start()
        pltpu.make_async_copy(gg_ref.at[0], send_ref, sem.at[1]).start()

    pltpu.make_async_copy(bg_ref, basis, sem.at[0]).wait()
    turned = basis[...].astype(F32).T
    empty = jnp.zeros((TILE, R), F32)
    rows = []
    for h in range(2):
        tiles = [turned[8 * t : 8 * t + 8] if t < 7 else empty for t in range(4 * h, 4 * h + 4)]
        rows.append(jnp.concatenate(tiles, axis=1))
    block = jnp.concatenate(rows, axis=0).astype(BF)
    block_ref[...] = jnp.broadcast_to(block[None], block_ref.shape)
    pltpu.make_async_copy(gg_ref.at[0], send_ref, sem.at[1]).wait()


def pack_kernel(sizes, gg_ref, gu_ref, other_ref, packed_ref, turned_ref, own, work, sem):
    core = lax.axis_index("outer")

    @pl.when(core == 0)
    def _():
        pltpu.make_async_copy(gg_ref.at[0], own, sem.at[0]).start()

    @pl.when(core != 0)
    def _():
        pltpu.make_async_copy(gu_ref.at[0], own, sem.at[0]).start()

    pltpu.make_async_copy(gg_ref.at[0], own, sem.at[0]).wait()
    empty = jnp.zeros((TILE, 2 * R), F32)

    @pl.loop(0, packed_ref.shape[0] // 256)
    def _(k):
        columns = pl.ds(pl.multiple_of(k * PERIOD, 128), PERIOD)
        x = jnp.concatenate(
            [own[:, columns].astype(F32), other_ref[:, columns].astype(F32)], axis=0
        )
        xt = x.T
        first = place(16 * k, sizes)
        for d in range(16):
            rows = []
            for h in range(2):
                tiles = []
                for t in range(4 * h, 4 * h + 4):
                    at = 8 * (7 * d + t)
                    tiles.append(xt[at : at + 8] if t < 7 else empty)
                rows.append(jnp.concatenate(tiles, axis=1))
            to = pl.multiple_of(16 * (first + place(d, sizes)), 16)
            work[pl.ds(to, 16), :] = jnp.concatenate(rows, axis=0).astype(BF)

    keep = pltpu.make_async_copy(work, packed_ref, sem.at[1])
    keep.start()

    @pl.loop(0, packed_ref.shape[0] // 256)
    def _(k):
        part = pl.ds(pl.multiple_of(k * 256, 256), 256)
        turned_ref[:, part] = work[part, :].astype(F32).T.astype(BF)

    keep.wait()


def products_kernel(far, basis_ref, turned_ref, packed_ref, sums_ref, left_ref, packed, sem):
    step = 512
    loads = []
    for k in range(packed_ref.shape[0] // step):
        part = pl.ds(k * step, step)
        loads.append(pltpu.make_async_copy(packed_ref.at[part], packed.at[part], sem.at[k]))
        loads[-1].start()
    partial = dot(turned_ref[...], basis_ref[...], 1, 0)
    group = groups((R, 128))
    total = jnp.zeros((R, 128), F32)
    for q in range(4):
        slab = partial[64 * q : 64 * q + R] + partial[64 * q + R : 64 * q + 64]
        total = total + jnp.where(group == q, slab, 0.0)
    total = total + pltpu.roll(total, 64, 1)
    total = total + pltpu.roll(total, 32, 1)
    left = (0.5 * total).astype(BF)
    left_ref[...] = left
    wide = left.astype(F32)
    pieces = []
    for q in range(4):
        one = jnp.where(group == q, wide, 0.0)
        pieces += [one, one]
    spread = jnp.concatenate(pieces, axis=0).astype(BF)
    for load in loads:
        load.wait()
    gram = dot(left, left, 0, 0)[0:R]
    terms = three_terms(jnp.where(group == 3, gram, 0.0))
    row = lax.broadcasted_iota(jnp.int32, (TILE, 128), 0)
    empty = jnp.zeros((TILE, 128), F32)
    extra = []
    for a in range(R // 2):
        tile = empty
        for s in range(6):
            at = 2 * a + s // 3
            tile = jnp.where(row == s, terms[s % 3][at : at + 1], tile)
        extra.append(tile)
    tiles = []
    for e in range(step // 16):
        tiles += [empty, extra[e % far]]
    added = jnp.concatenate(tiles, axis=0)
    for k in range(len(loads)):
        out = dot(packed[pl.ds(k * step, step), :], spread, 1, 0)
        sums_ref[pl.ds(k * step, step), :] = (out + added).astype(BF)


def summed(parts_ref, scale):
    count, rows, _ = parts_ref.shape

    def add(k, acc):
        return acc + parts_ref[k].astype(F32)

    acc = lax.fori_loop(0, count, add, jnp.zeros((rows, 128), F32), unroll=4)
    acc = acc.reshape(rows // 16, 16, 128)
    row = lax.broadcasted_iota(jnp.int32, acc.shape, 1)
    lane = lax.broadcasted_iota(jnp.int32, acc.shape, 2)
    term = jnp.zeros_like(acc)
    for first in (8, 11):
        gram = acc[:, first : first + 1] + acc[:, first + 1 : first + 2] + acc[:, first + 2 : first + 3]
        for s, part in enumerate(three_terms(gram)):
            term = jnp.where(row == first + s, part, term)
    out = jnp.where((row >= 8) & (lane >= 96), term, scale * acc)
    return out.reshape(rows, 128)


def halfway_kernel(parts_ref, out_ref):
    out_ref[...] = summed(parts_ref, 1.0).astype(BF)


def total_kernel(parts_ref, block_ref, kept_ref):
    out = summed(parts_ref, 0.5)
    block_ref[...] = jnp.broadcast_to(out.astype(BF)[None], block_ref.shape)
    kept_ref[...] = out


def pick(core, first, second, to, sem, start):
    if not start:
        pltpu.make_async_copy(first, to, sem).wait()
        return

    @pl.when(core == 0)
    def _():
        pltpu.make_async_copy(first, to, sem).start()

    @pl.when(core != 0)
    def _():
        pltpu.make_async_copy(second, to, sem).start()


def solve_kernel(
    line_ref, kept_ref, left_ref, gg_ref, gu_ref, out_ref, grad_ref, other_grad_ref, tiles, grams, sem
):
    core = lax.axis_index("outer")
    pick(core, gg_ref.at[0], gu_ref.at[0], grad_ref, sem.at[0], True)
    pick(core, gu_ref.at[0], gg_ref.at[0], other_grad_ref, sem.at[1], True)
    high = lax.Precision.HIGHEST
    group = groups((R, 128))
    row = lax.broadcasted_iota(jnp.int32, (R, 128), 0)
    lane = lax.broadcasted_iota(jnp.int32, (R, 128), 1)
    half = R // 2
    for f in range(half):
        tiles[8 * f : 8 * f + 8] = line_ref[16 * f : 16 * f + 16].astype(F32)[8:16]
    for odd in range(2):
        gram = tiles[pl.ds(3 * odd, half, stride=8), :]
        for s in range(1, 3):
            gram = gram + tiles[pl.ds(3 * odd + s, half, stride=8), :]
        grams[pl.ds(odd, half, stride=2), :] = gram
    m = jnp.where(group == 0, pltpu.roll(grams[0:R], 32, 1), 0.0)
    m = jnp.where((group == 1) & (row == lane % R), 1.0, m)
    pivots = jnp.ones((R, 128), F32)
    for first in range(0, R, BLOCK):
        columns = [jnp.broadcast_to(m[:, k : k + 1], (R, 128)) for k in range(first, first + BLOCK)]
        rows = [m[k : k + 1] for k in range(first, first + BLOCK)]
        for i in range(BLOCK):
            k = first + i
            pivot = columns[i][k : k + 1]
            pivots = jnp.where(row == k, pivot, pivots)
            factor = jnp.where(row > k, columns[i] * (1.0 / pivot), 0.0)
            for j in range(i + 1, BLOCK):
                columns[j] = columns[j] - factor * columns[j][k : k + 1]
                at = first + j
                rows[j] = rows[j] - factor[at : at + 1] * rows[i]
            m = m - factor * rows[i]
    scale = lax.rsqrt(pivots)
    scale = scale * (1.5 - 0.5 * pivots * scale * scale)
    one = jnp.where(group == 1, m * scale, 0.0)
    one = one + pltpu.roll(one, 64, 1)
    one = one + pltpu.roll(one, 32, 1)
    u = kept_ref[...]
    rows = []
    for t in range(7):
        h, q = divmod(t, 4)
        rows.append(jnp.where(groups((TILE, 128)) == q, u[8 * h : 8 * h + 8], 0.0))
    rows.append(jnp.zeros((128 - W, 128), F32))
    nexts = dot(one, jnp.concatenate(rows, axis=0), 1, 1, high)
    left = jnp.where(group == 0, left_ref[...].astype(F32), 0.0)
    tall = jnp.concatenate([one, one, one, one], axis=0)
    factors = dot(left, tall, 1, 1, high)
    out_ref[0:R] = jnp.where(lane < 64, nexts, factors)
    out_ref[R : 2 * R] = dot(factors[:, 0:R], one, 1, 0, high)
    pick(core, gg_ref.at[0], gu_ref.at[0], grad_ref, sem.at[0], False)
    pick(core, gu_ref.at[0], gg_ref.at[0], other_grad_ref, sem.at[1], False)


CUTS = (4, 7, 8)


def residual(sizes, sums_ref, side, grad, resid, gate, up, at, sem):
    top = side.astype(BF)
    rest = (side - top.astype(F32)).astype(BF)
    side = jnp.concatenate([top, rest], axis=0)
    none = jnp.zeros_like(side)
    side = jnp.concatenate(
        [jnp.concatenate([side, none], axis=1), jnp.concatenate([none, side], axis=1)], axis=0
    )
    pair_group = groups((16, 128))
    second = lax.broadcasted_iota(jnp.int32, (16, 128), 0) >= 8
    masks = []
    for v in range(7):
        a, b = (2 * v) % 7, (2 * v + 1) % 7
        masks.append(jnp.where(pair_group == jnp.where(second, b % 4, a % 4), 1.0, 0.0).astype(BF))
    wide = 2 * PERIOD
    steps = sums_ref.shape[0] // 512
    edges = [0, *(e * steps // 8 for e in CUTS)]
    parts = [pl.ds(a * wide, (b - a) * wide) for a, b in zip(edges, edges[1:]) if b > a]
    spans = [range(a, b) for a, b in zip(edges, edges[1:]) if b > a]
    for cut, part in enumerate(parts):
        for k in spans[cut]:
            halves = []
            for half in range(2):
                tiles = []
                for d in range(32 * k + 16 * half, 32 * k + 16 * half + 16):
                    at_d = 16 * place(d, sizes)
                    x = sums_ref[at_d : at_d + 16, :]
                    tiles += [x[0:8]] * 4 + [x[8:16]] * 3
                rows = []
                for v in range(56):
                    pair = jnp.concatenate(tiles[2 * v : 2 * v + 2], axis=0)
                    rows.append(pair * masks[v % 7])
                halves.append(jnp.concatenate(rows, axis=0))
            both = dot(side, jnp.concatenate(halves, axis=1), 1, 1)
            for half in range(2):
                product = both[64 * half : 64 * half + R] + both[64 * half + R : 64 * half + 64]
                columns = pl.ds(k * wide + half * PERIOD, PERIOD)
                resid[:, columns] = (grad[:, columns].astype(F32) - product).astype(BF)

        @pl.when(at == 0)
        def _():
            pltpu.make_async_copy(resid.at[:, part], gate.at[0, :, part], sem.at[cut]).start()

        @pl.when(at != 0)
        def _():
            pltpu.make_async_copy(resid.at[:, part], up.at[0, :, part], sem.at[cut]).start()

    for cut, part in enumerate(parts):
        pltpu.make_async_copy(resid.at[:, part], gate.at[0, :, part], sem.at[cut]).wait()


def own_kernel(
    sizes, sums_ref, own_ref, other_ref, grad,
    ng_ref, nu_ref, fg_ref, fu_ref, rg_ref, ru_ref, resid, sem_out,
):
    core = lax.axis_index("outer")
    own, other = own_ref[0:R], other_ref[0:R]
    gate, up = jnp.where(core == 0, own, other), jnp.where(core == 0, other, own)
    ng_ref[...] = gate[:, 0:W]
    nu_ref[...] = up[:, 0:W]
    fg_ref[...] = gate[:, 64 : 64 + R]
    fu_ref[...] = up[:, 64 : 64 + R]
    residual(sizes, sums_ref, own_ref[R : 2 * R], grad, resid, rg_ref, ru_ref, core, sem_out)


def other_kernel(sizes, sums_ref, other_ref, grad, rg_in, ru_in, rg_ref, ru_ref, resid, sem_out):
    del rg_in, ru_in
    core = lax.axis_index("outer")
    residual(sizes, sums_ref, other_ref[R : 2 * R], grad, resid, rg_ref, ru_ref, 1 - core, sem_out)


def call(kernel, outs, scratch, spaces_in, spaces_out, cost, limit, aliases={}):
    space = {"h": pltpu.HBM, "v": pltpu.VMEM}
    specs_out = tuple(pl.BlockSpec(memory_space=space[s]) for s in spaces_out)
    run = pl.pallas_call(
        kernel,
        out_shape=[
            pltpu.HBM(o.shape, o.dtype) if s == "h" and not INTERPRET else o
            for s, o in zip(spaces_out, outs)
        ],
        in_specs=[pl.BlockSpec(memory_space=space[s]) for s in spaces_in],
        out_specs=specs_out,
        scratch_shapes=scratch,
        input_output_aliases=aliases,
        cost_estimate=pl.CostEstimate(flops=cost, bytes_accessed=cost // 16, transcendentals=0),
        compiler_params=pltpu.CompilerParams(vmem_limit_bytes=limit << 20),
        interpret=INTERPRET,
    )

    def pinned(*args):
        return run(
            *(
                pltpu.with_memory_space_constraint(x, pltpu.HBM) if s == "h" and not INTERPRET else x
                for s, x in zip(spaces_in, args)
            )
        )

    return pinned


def shape(dims, dtype):
    return jax.ShapeDtypeStruct(dims, dtype)


def local(grad_gate, grad_up, basis_gate, basis_up):
    sizes = tuple(lax.axis_size(a) for a in ROW)
    near, far = lax.axis_size(NEAR), lax.axis_size(FAR)
    columns = grad_gate.shape[2]
    packed_rows = 16 * near * far
    swap = [(0, 1), (1, 0)]
    dma = pltpu.SemaphoreType.DMA

    def exchange(x, axes):
        return lax.all_to_all(x, axes, 0, 0, tiled=True)

    def gather_far(block):
        return exchange(block, FAR).reshape(16 * far, 128)

    def gather_near(line):
        copies = jnp.broadcast_to(line[None], (near, 16 * far, 128))
        return exchange(copies, NEAR).reshape(packed_rows, 128)

    block, send = call(
        prepare_kernel,
        (shape((far, 16, 128), BF), shape((R, columns), BF)),
        [pltpu.VMEM((R, W), BF), dma((2,))],
        "hhhh",
        "vv",
        1 << 20,
        6,
    )(basis_gate, basis_up, grad_gate, grad_up)
    other = lax.ppermute(send, "outer", swap)
    packed, turned = call(
        functools.partial(pack_kernel, sizes),
        (shape((packed_rows, 256), BF), shape((256, packed_rows), BF)),
        [pltpu.VMEM((R, columns), BF), pltpu.VMEM((packed_rows, 256), BF), dma((2,))],
        "hhv",
        "hv",
        1 << 26,
        16,
    )(grad_gate, grad_up, other)
    basis = gather_near(gather_far(block))
    sums, left = call(
        functools.partial(products_kernel, far),
        (shape((packed_rows, 128), BF), shape((R, 128), BF)),
        [pltpu.VMEM((packed_rows, 256), BF), dma((packed_rows // 512,))],
        "vvh",
        "vv",
        1 << 26,
        16,
    )(basis, turned, packed)
    parts = exchange(sums.reshape(near, 16 * far, 128), NEAR)
    (halfway,) = call(halfway_kernel, (shape((16 * far, 128), BF),), [], "v", "v", 1 << 20, 8)(parts)
    parts = exchange(halfway.reshape(far, 16, 128), FAR)
    block, kept = call(
        total_kernel,
        (shape((far, 16, 128), BF), shape((16, 128), F32)),
        [],
        "v",
        "vv",
        1 << 20,
        4,
    )(parts)
    line = gather_far(block)
    natural = shape((R, columns), BF)
    own, own_grad, other_grad = call(
        solve_kernel,
        (shape((2 * R, 128), F32), natural, natural),
        [pltpu.VMEM((136, 128), F32), pltpu.VMEM((R + 8, 128), F32), dma((2,))],
        "vvvhh",
        "vvv",
        1 << 26,
        4,
    )(line, kept, left, grad_gate, grad_up)
    other = lax.ppermute(own, "outer", swap)
    sums, other = lax.optimization_barrier((gather_near(line), other))
    sums_other = lax.ppermute(sums, "outer", swap)
    working = pltpu.VMEM((R, columns), BF)
    resids = (shape(grad_gate.shape, BF), shape(grad_gate.shape, BF))
    *small, rg, ru = call(
        functools.partial(own_kernel, sizes),
        (shape((R, W), F32), shape((R, W), F32), shape((R, R), F32), shape((R, R), F32), *resids),
        [working, dma((len(CUTS),))],
        "vvvv",
        "vvvvhh",
        1 << 26,
        12,
    )(sums, own, other, own_grad)
    rg, ru = call(
        functools.partial(other_kernel, sizes),
        resids,
        [working, dma((len(CUTS),))],
        "vvvhh",
        "hh",
        1 << 26,
        12,
        {3: 0, 4: 1},
    )(sums_other, other, other_grad, rg, ru)
    return (*small, rg, ru)


def solution(mesh):
    rows = mesh.shape["row"]
    sizes = (4, 2, 4, 2, 4) if rows == 256 else (4, 1, 4, 1, rows // 16)
    finer = Mesh(mesh.devices.reshape(mesh.shape["outer"], *sizes), ("outer", *ROW))
    return jax.shard_map(
        local,
        mesh=finer,
        in_specs=(P("outer", ROW, None), P("outer", ROW, None), P(None, ROW), P(None, ROW)),
        out_specs=(
            P(None, ROW), P(None, ROW), P(ROW, None), P(ROW, None),
            P("outer", ROW, None), P("outer", ROW, None),
        ),
        check_vma=False,
    )
```
